128 devices in a mesh: gx: 8 (over z, core), gy: 16 (over x, y).
Axes of the slice: x: 4, y: 4, z: 4, core: 2. Of those that a mesh axis runs over, the one named last changes fastest.
Arguments:
- velocity: float32 [3, 768, 256, 128], P(None, 'gx', 'gy'), may hold values from -6 to 6
- states: float32 [2, 768, 256, 128], P(None, 'gx', 'gy'), may hold values from -6 to 6
- pull_plan: int32 [48, 16], P('gx', 'gy'), may hold values from 0 to 31, as said below
- send_plan: int32 [8, 16, 16, 2], P('gx', 'gy'), may hold values from -1 to 5, as said below
- codes: int32 [3, 48, 16], P(None, 'gx', 'gy'), may hold values from 0 to 1023, as said below
Outputs:
- hessian_velocity: float32 [3, 768, 256, 128], P(None, 'gx', 'gy')
The draws below stay inside these ranges and needn't reach their ends.
Inputs may be any that keep to these rules, and one draw needn't show every extreme that they name: `pull_plan`: the bricks of one device name distinct slots; slot p of device (g, h) is filled by device (g, p // 2) along gy. Every device uses 2 slots from at least one supplying device, and at most 2 from any. send_plan[g, s, h, e] is the brick of device (g, s), in order of brick rows then brick columns within the device, that fills slot s * 2 + e of device (g, h), or -1 where no brick of device (g, h) names that slot; it agrees with pull_plan. codes[0] and codes[1] lie in 0 .. 7; codes[2] is the depth position in units of 1 / 8 cell.
All inputs are finite; a program needn't handle non-finite values.
Results may differ from the reference program's by a relative error of at most 0.00013.
Values sent between devices are 32-bit elements; how exact they have to be, the bound alone decides.
No kernel may reach another device: no remote copies, remote signals or barrier semaphores. Data moves between devices by JAX's collectives and lax.ppermute only.
A program may use at most 128 MiB of HBM per device.

```python
import jax
import jax.numpy as jnp
from jax import lax

CX = 96
CY = 16
CZ = 128
BX = 16
BY = 16
CAP = 2
QF = 8
STEPS = 2
NX = 768
NY = 256
BRX_DEV = 6
BRY_DEV = 1
BRX = 48
BRY = 16
GX_DEVS = 8
GY_DEVS = 16


def plan_tables(key):
    base = jax.random.fold_in(key, 11)
    key_hot, key_noise, key_pairs, key_local, key_order = jax.random.split(base, 5)
    bricks = CX // BX * (CY // BY)
    lowest = max(1, -(-(bricks - GY_DEVS) // (CAP - 1)))
    highest = bricks // CAP
    hotness = jax.random.randint(key_hot, (GX_DEVS, 1, GY_DEVS), 0, 64)
    jitter = jax.random.randint(key_noise, (GX_DEVS, GY_DEVS, GY_DEVS), 0, 32)
    favour = jnp.zeros((GX_DEVS, GY_DEVS, GY_DEVS), jnp.int32).at[:, 0, GY_DEVS - 1].set(1000)
    ranking = (hotness + jitter + favour) * GY_DEVS + jnp.arange(GY_DEVS, dtype=jnp.int32)[None, None, :]
    wanted = bricks - lowest * (CAP - 1)
    _, ranked = lax.top_k(ranking, wanted)
    ranked = ranked.astype(jnp.int32)
    doubled = jax.random.randint(key_pairs, (GX_DEVS, GY_DEVS, 1), lowest, highest + 1)
    brick_order = jnp.arange(bricks, dtype=jnp.int32)[None, None, :]
    grouped = brick_order < CAP * doubled
    position = jnp.where(grouped, brick_order // CAP, brick_order - doubled * (CAP - 1))
    slot_number = jnp.where(grouped, brick_order % CAP, 0)
    supplier = jnp.take_along_axis(ranked, position, axis=2)
    local_brick = jax.random.randint(key_local, (GX_DEVS, GY_DEVS, bricks), 0, bricks)
    local_brick = local_brick.at[0, 0, 0].set(bricks - 1)
    pulled = supplier * CAP + slot_number
    shuffles = jax.vmap(lambda subkey: jax.random.permutation(subkey, bricks))(jax.random.split(key_order, GX_DEVS * GY_DEVS)).reshape(GX_DEVS, GY_DEVS, bricks)
    pulled = jnp.take_along_axis(pulled, shuffles.astype(jnp.int32), axis=2)
    pull_grid = pulled.reshape(GX_DEVS, GY_DEVS, CX // BX, CY // BY).transpose(0, 2, 1, 3)
    pull_grid = pull_grid.reshape(GX_DEVS * (CX // BX), GY_DEVS * (CY // BY))
    matches = (supplier[:, None, :, None, :] == jnp.arange(GY_DEVS, dtype=jnp.int32)[None, :, None, None, None]) & (slot_number[:, None, :, None, :] == jnp.arange(CAP, dtype=jnp.int32)[None, None, None, :, None])
    sending = jnp.sum(jnp.where(matches, local_brick[:, None, :, None, :] + 1, 0), axis=4) - 1
    return (pull_grid.astype(jnp.int32), sending.astype(jnp.int32))


def draw_pull_plan(key, part):
    return plan_tables(key)[0]


def draw_send_plan(key, part):
    return plan_tables(key)[1]


def draw_codes(key, part):
    base = jax.random.fold_in(key, 23)
    key_fine, key_depth = jax.random.split(base, 2)
    fine = jax.random.randint(key_fine, (2, BRX, BRY), 0, QF)
    fine = fine.at[1, 0, 0].set(0)
    deep = jax.random.randint(key_depth, (1, BRX, BRY), 0, CZ * QF)
    deep = deep.at[0, 0, 0].set(CZ * QF - 1)
    return jnp.concatenate([fine, deep], axis=0).astype(jnp.int32)


def block_scale(stream_key, shape, pieces, smallest, top_value):
    def one(dim, blocks):
        draws = jax.random.uniform(jax.random.fold_in(jax.random.fold_in(stream_key, 6), dim), (blocks,), jnp.float32, smallest / len(pieces), top_value / len(pieces))
        return jnp.repeat(jnp.exp(draws), shape[dim] // blocks).reshape((-1,) + (1,) * (len(shape) - dim - 1))

    gain = one(*pieces[0])
    for cut in pieces[1:]:
        gain = gain * one(*cut)
    return gain


def noise(rng, shape, deviation, reach, cuts=(), kind=jnp.bfloat16):
    drawn = jax.random.normal(rng, shape, jnp.float32) * deviation
    if len(cuts) > 0:
        drawn = block_scale(rng, shape, cuts, -0.22, 0.18) * drawn
    return jnp.clip(drawn, min=-reach, max=reach).astype(kind)


def setup_inputs(seed: int = 0) -> dict:
    key_list = jax.random.split(jax.random.key(seed), 6)
    return {
        "velocity": noise(key_list[0], (3, NX, NY, CZ), 1.0, 6.0, ((1, 8), (2, 16)), jnp.float32),
        "states": noise(key_list[1], (STEPS, NX, NY, CZ), 1.0, 6.0, ((1, 8), (2, 16)), jnp.float32),
        "pull_plan": draw_pull_plan(jax.random.fold_in(key_list[5], 71), 0),
        "send_plan": draw_send_plan(jax.random.fold_in(key_list[5], 71), 0),
        "codes": draw_codes(jax.random.fold_in(key_list[5], 71), 0),
    }


def cubic_weights(fraction):
    return (-fraction * (fraction - 1.0) * (fraction - 2.0) / 6.0,
            (fraction + 1.0) * (fraction - 1.0) * (fraction - 2.0) / 2.0,
            -(fraction + 1.0) * fraction * (fraction - 2.0) / 2.0,
            (fraction + 1.0) * fraction * (fraction - 1.0) / 6.0)


def band_matrix(code_row, cells):
    fraction = code_row.astype(jnp.float32) / QF
    weights = cubic_weights(fraction[:, None, None])
    row_index = jnp.arange(cells)[None, :, None]
    col_index = jnp.arange(cells + 3)[None, None, :]
    total = jnp.zeros((code_row.shape[0], cells, cells + 3), jnp.float32)
    for offset in range(4):
        total = total + weights[offset] * (col_index == row_index + offset).astype(jnp.float32)
    return total


def circulant(code_row, cells):
    shift_cells = code_row // QF
    fraction = (code_row % QF).astype(jnp.float32) / QF
    weights = cubic_weights(fraction[:, None, None])
    row_index = jnp.arange(cells)[None, :, None]
    col_index = jnp.arange(cells)[None, None, :]
    total = jnp.zeros((code_row.shape[0], cells, cells), jnp.float32)
    for offset in range(4):
        target = (row_index + shift_cells[:, None, None] + offset - 1) % cells
        total = total + weights[offset] * (col_index == target).astype(jnp.float32)
    return total


def interpolate(windows, weight_rows, weight_cols, weight_depth):
    high = lax.Precision.HIGHEST
    along_depth = jnp.einsum("nabz,ncz->nabc", windows, weight_depth, precision=high)
    along_rows = jnp.einsum("nia,nabc->nibc", weight_rows, along_depth, precision=high)
    return jnp.einsum("njb,nibc->nijc", weight_cols, along_rows, precision=high)


def interpolate_adjoint(values, weight_rows, weight_cols, weight_depth):
    high = lax.Precision.HIGHEST
    along_cols = jnp.einsum("njb,nijc->nibc", weight_cols, values, precision=high)
    along_rows = jnp.einsum("nia,nibc->nabc", weight_rows, along_cols, precision=high)
    return jnp.einsum("ncz,nabc->nabz", weight_depth, along_rows, precision=high)


def gradient(field):
    parts = []
    for axis_number in range(3):
        parts.append((jnp.roll(field, -1, axis_number) - jnp.roll(field, 1, axis_number)) * 0.5)
    return jnp.stack(parts)


def reference(velocity, states, pull_plan, send_plan, codes):
    brick_a = jnp.arange(BRX)[:, None]
    brick_b = jnp.arange(BRY)[None, :]
    source_gy = pull_plan // CAP
    slot_number = pull_plan % CAP
    owner_gx = brick_a // BRX_DEV
    owner_gy = brick_b // BRY_DEV
    local_brick = send_plan[owner_gx, source_gy, owner_gy, slot_number]
    first_row = (owner_gx * BRX_DEV + local_brick // BRY_DEV) * BX
    first_col = (source_gy * BRY_DEV + local_brick % BRY_DEV) * BY
    row_index = (first_row[:, :, None] - 1 + jnp.arange(BX + 3)[None, None, :]) % NX
    col_index = (first_col[:, :, None] - 1 + jnp.arange(BY + 3)[None, None, :]) % NY
    rows_full = row_index[:, :, :, None]
    cols_full = col_index[:, :, None, :]
    count = BRX * BRY
    weight_rows = band_matrix(codes[0].reshape(count), BX)
    weight_cols = band_matrix(codes[1].reshape(count), BY)
    weight_depth = circulant(codes[2].reshape(count), CZ)

    def pull(field):
        windows = field[rows_full, cols_full].reshape(count, BX + 3, BY + 3, CZ)
        values = interpolate(windows, weight_rows, weight_cols, weight_depth)
        return values.reshape(BRX, BRY, BX, BY, CZ).transpose(0, 2, 1, 3, 4).reshape(NX, NY, CZ)

    def push(field):
        values = field.reshape(BRX, BX, BRY, BY, CZ).transpose(0, 2, 1, 3, 4).reshape(count, BX, BY, CZ)
        windows = interpolate_adjoint(values, weight_rows, weight_cols, weight_depth)
        windows = windows.reshape(BRX, BRY, BX + 3, BY + 3, CZ)
        return jnp.zeros((NX, NY, CZ), jnp.float32).at[rows_full, cols_full].add(windows)

    step_size = 1.0 / STEPS
    gradients = [gradient(states[step]) for step in range(STEPS)]
    tangent = jnp.zeros((NX, NY, CZ), jnp.float32)
    for step in range(STEPS):
        tangent = pull(tangent - step_size * jnp.sum(velocity * gradients[step], axis=0))
    adjoint = tangent
    force = jnp.zeros((3, NX, NY, CZ), jnp.float32)
    for step in reversed(range(STEPS)):
        adjoint = push(adjoint)
        force = force - step_size * adjoint[None] * gradients[step]
    return force
```

```python
import functools

import jax
import jax.numpy as jnp
import numpy as np
from jax import lax
from jax.experimental import pallas as pl
from jax.experimental.pallas import tpu as pltpu
from jax.sharding import PartitionSpec as P

QF = 8
PEERS = 16
RB = 12
BRICKS = 6


def weights_of(f):
    return np.array(
        [
            -f * (f - 1.0) * (f - 2.0) / 6.0,
            (f + 1.0) * (f - 1.0) * (f - 2.0) / 2.0,
            -(f + 1.0) * f * (f - 2.0) / 2.0,
            (f + 1.0) * f * (f - 1.0) / 6.0,
        ]
    )


WEIGHTS = np.stack([weights_of(k / QF) for k in range(QF)])
PAIRS = np.stack([[np.dot(w[: 4 - d], w[d:]) for d in range(4)] for w in WEIGHTS])

VMEM = pl.BlockSpec(memory_space=pltpu.VMEM)
SMEM = pl.BlockSpec(memory_space=pltpu.SMEM)
F32 = jnp.float32


def params(mib=48):
    return pltpu.CompilerParams(vmem_limit_bytes=mib * 1024 * 1024)


def turned_shape(lead=PEERS):
    return jax.ShapeDtypeStruct((lead, RB, 8, 128), F32)


def gradients(st, top, bottom, left, right, rb, k):
    rows = pl.ds(rb * 8, 8)
    x = st[k, rows]
    before = st[k, jnp.maximum(rb * 8 - 1, 0)]
    before = jnp.where(rb == 0, top[k], before)
    after = st[k, jnp.minimum(rb * 8 + 8, 95)]
    after = jnp.where(rb == RB - 1, bottom[k], after)
    up = jnp.concatenate([x[1:], after[None]], axis=0)
    down = jnp.concatenate([before[None], x[:-1]], axis=0)
    col = lax.broadcasted_iota(jnp.int32, x.shape, 1)
    lo = left[k, rows][:, None, :]
    hi = right[k, rows][:, None, :]
    nxt = jnp.where(col == 15, hi, pltpu.roll(x, 15, 1))
    prv = jnp.where(col == 0, lo, pltpu.roll(x, 1, 1))
    return (
        (up - down) * 0.5,
        (nxt - prv) * 0.5,
        (pltpu.roll(x, 127, 2) - pltpu.roll(x, 1, 2)) * 0.5,
    )


def source_kernel(k, v, st, top, bottom, left, right, out):
    g = gradients(st, top, bottom, left, right, pl.program_id(0), k)
    a = -0.5 * (v[0] * g[0] + v[1] * g[1] + v[2] * g[2])
    out[:, 0] = a.reshape(128, 128).T.reshape(PEERS, 8, 128)


def whole(shape):
    return pl.BlockSpec(shape, lambda i: (0,) * len(shape))


STATE_SPECS = [
    whole((2, 96, 16, 128)),
    whole((2, 16, 128)),
    whole((2, 16, 128)),
    whole((2, 96, 128)),
    whole((2, 96, 128)),
]
NATURAL3 = pl.BlockSpec((3, 8, 16, 128), lambda i: (0, i, 0, 0))
TURNED = pl.BlockSpec((PEERS, 1, 8, 128), lambda i: (0, i, 0, 0))


def source(k, velocity, state_args):
    return pl.pallas_call(
        functools.partial(source_kernel, k),
        grid=(RB,),
        in_specs=[NATURAL3] + STATE_SPECS,
        out_specs=TURNED,
        out_shape=turned_shape(),
        compiler_params=params(),
        name="source%d" % k,
    )(velocity, *state_args)


def force_kernel(adj1, adj0, st, top, bottom, left, right, out):
    rb = pl.program_id(0)
    b1 = (adj1[:, 0].reshape(128, 128).T * -0.5).reshape(8, 16, 128)
    b0 = (adj0[:, 0].reshape(128, 128).T * -0.5).reshape(8, 16, 128)
    g1 = gradients(st, top, bottom, left, right, rb, 1)
    g0 = gradients(st, top, bottom, left, right, rb, 0)
    for c in range(3):
        out[c] = b1 * g1[c] + b0 * g0[c]


def force(adj1, adj0, state_args):
    return pl.pallas_call(
        force_kernel,
        grid=(RB,),
        in_specs=[TURNED, TURNED] + STATE_SPECS,
        out_specs=NATURAL3,
        out_shape=jax.ShapeDtypeStruct((3, 96, 16, 128), F32),
        compiler_params=params(),
        name="force",
    )(adj1, adj0, *state_args)


def lanes():
    return lax.broadcasted_iota(jnp.int32, (8, 128), 1)


def column_taps(x):
    col = lax.broadcasted_iota(jnp.int32, x.shape, 2) % 16
    up = pltpu.roll(x, 16, 2)
    dn = pltpu.roll(x, 112, 2)
    after = jnp.concatenate([up[1:], up[:1]], axis=0)
    before = jnp.concatenate([dn[-1:], dn[:-1]], axis=0)
    return (
        pltpu.roll(jnp.where(col == 15, before, x), 1, 2),
        x,
        pltpu.roll(jnp.where(col == 0, after, x), 127, 2),
        pltpu.roll(jnp.where(col < 2, after, x), 126, 2),
    )


def column_taps_adjoint(t0, t1, t2, t3):
    col = lax.broadcasted_iota(jnp.int32, t1.shape, 2) % 16
    p0 = pltpu.roll(t0, 127, 2)
    p2 = pltpu.roll(t2, 1, 2)
    p3 = pltpu.roll(t3, 2, 2)
    own = t1 + jnp.where(col == 15, 0.0, p0) + jnp.where(col == 0, 0.0, p2) + jnp.where(col < 2, 0.0, p3)
    after = jnp.where(col == 0, p2, 0.0) + jnp.where(col < 2, p3, 0.0)
    before = jnp.where(col == 15, p0, 0.0)
    after = pltpu.roll(after, 112, 2)
    before = pltpu.roll(before, 16, 2)
    after = jnp.concatenate([after[-1:], after[:-1]], axis=0)
    before = jnp.concatenate([before[1:], before[:1]], axis=0)
    return own + after + before


def fill_taps(taps, e, x):
    for t, y in enumerate(column_taps(x)):
        taps[t, :, e] = y


def brick_plan(tab, wt, d, k):
    p = tab[d, 32 + k]
    s = p // 2
    l = tab[s, d * 2 + p % 2]
    wr = [wt[tab[d, 38 + k], t] for t in range(4)]
    wc = [wt[tab[d, 44 + k], t] for t in range(4)]
    return s, l, wr, wc


def brick_forward(taps, s, l, wr, wc):
    lane = lanes()
    c = []
    for i in range(4):
        e = 2 * l + i
        acc = wc[0] * taps[0, s, e]
        for t in range(1, 4):
            acc = acc + wc[t] * taps[t, s, e]
        c.append(acc)
    outs = []
    for h in range(2):
        prv, cur, nxt = c[h], c[h + 1], c[h + 2]
        outs.append(
            wr[0] * pltpu.roll(jnp.where(lane >= 112, prv, cur), 16, 1)
            + wr[1] * cur
            + wr[2] * pltpu.roll(jnp.where(lane < 16, nxt, cur), 112, 1)
            + wr[3] * pltpu.roll(jnp.where(lane < 32, nxt, cur), 96, 1)
        )
    return outs


def brick_adjoint(acc, s, l, wr, wc, v):
    lane = lanes()
    zero = jnp.zeros((8, 128), F32)
    c = [zero, zero, zero, zero]
    for h in range(2):
        p0 = wr[0] * pltpu.roll(v[h], 112, 1)
        p2 = wr[2] * pltpu.roll(v[h], 16, 1)
        p3 = wr[3] * pltpu.roll(v[h], 32, 1)
        c[h] = c[h] + jnp.where(lane >= 112, p0, 0.0)
        c[h + 1] = (
            c[h + 1]
            + wr[1] * v[h]
            + jnp.where(lane >= 112, 0.0, p0)
            + jnp.where(lane < 16, 0.0, p2)
            + jnp.where(lane < 32, 0.0, p3)
        )
        c[h + 2] = c[h + 2] + jnp.where(lane < 16, p2, 0.0) + jnp.where(lane < 32, p3, 0.0)
    for i in range(4):
        e = 2 * l + i
        for t in range(4):
            acc[t, s, e] = acc[t, s, e] + wc[t] * c[i]


def pull_kernel(tab, wt, x, prv, nxt, out, taps):
    fill_taps(taps, 0, prv[...])
    fill_taps(taps, RB + 1, nxt[...])

    @pl.loop(0, RB)
    def _(rb):
        fill_taps(taps, rb + 1, x[:, rb])

    @pl.loop(0, PEERS)
    def _(d):
        for k in range(BRICKS):
            o = brick_forward(taps, *brick_plan(tab, wt, d, k))
            for h in range(2):
                out[d, 2 * k + h] = o[h]


TAPS = pltpu.VMEM((4, PEERS, RB + 2, 8, 128), F32)


def pull(tab, wt, x, prv, nxt):
    return pl.pallas_call(
        pull_kernel,
        in_specs=[SMEM, SMEM, VMEM, VMEM, VMEM],
        out_specs=VMEM,
        out_shape=turned_shape(),
        scratch_shapes=[TAPS],
        compiler_params=params(),
        name="pull",
    )(tab, wt, x, prv, nxt)


def clear(acc):
    @pl.loop(0, RB + 2)
    def _(e):
        acc[:, :, e] = jnp.zeros((4, PEERS, 8, 128), F32)


def spill(acc, out, lo, hi):
    def gather(e):
        return column_taps_adjoint(*[acc[t, :, e] for t in range(4)])

    lo[...] = gather(0)
    hi[...] = gather(RB + 1)

    @pl.loop(0, RB)
    def _(rb):
        out[:, rb] = gather(rb + 1)


def push_kernel(tab, wt, v, out, lo, hi, acc):
    clear(acc)

    @pl.loop(0, PEERS)
    def _(d):
        for k in range(BRICKS):
            brick_adjoint(acc, *brick_plan(tab, wt, d, k), [v[d, 2 * k], v[d, 2 * k + 1]])

    spill(acc, out, lo, hi)


EDGE = jax.ShapeDtypeStruct((PEERS, 8, 128), F32)


def push(tab, wt, v):
    return pl.pallas_call(
        push_kernel,
        in_specs=[SMEM, SMEM, VMEM],
        out_specs=[VMEM, VMEM, VMEM],
        out_shape=[turned_shape(), EDGE, EDGE],
        scratch_shapes=[TAPS],
        compiler_params=params(),
        name="push",
    )(tab, wt, v)


def normal_kernel(tab, wt, kt, x, prv, nxt, out, lo, hi, taps, acc):
    clear(acc)
    for q in range(2):
        fill_taps(taps.at[q], 0, prv[:, q])
        fill_taps(taps.at[q], RB + 1, nxt[:, q])

    @pl.loop(0, RB)
    def _(rb):
        for q in range(2):
            fill_taps(taps.at[q], rb + 1, x[:, q, rb])

    @pl.loop(0, PEERS)
    def _(d):
        sub = lax.broadcasted_iota(jnp.int32, (8, 128), 0)
        for k in range(BRICKS):
            plan = brick_plan(tab, wt, d, k)
            f = tab[d, 50 + k] % QF
            t0 = brick_forward(taps.at[0], *plan)
            t1 = brick_forward(taps.at[1], *plan)
            v = []
            for h in range(2):

                def plane(a):
                    return pltpu.roll(jnp.where(sub >= a, t0[h], t1[h]), 8 - a, 0)

                y = kt[f, 0] * plane(4)
                for dd in range(1, 4):
                    y = y + kt[f, dd] * (plane(4 - dd) + plane(4 + dd))
                v.append(y)
            brick_adjoint(acc, *plan, v)

    spill(acc, out, lo, hi)


def normal(tab, wt, kt, x, prv, nxt):
    return pl.pallas_call(
        normal_kernel,
        in_specs=[SMEM, SMEM, SMEM, VMEM, VMEM, VMEM],
        out_specs=[VMEM, VMEM, VMEM],
        out_shape=[turned_shape(), EDGE, EDGE],
        scratch_shapes=[pltpu.VMEM((2, 4, PEERS, RB + 2, 8, 128), F32), TAPS],
        compiler_params=params(),
        name="normal",
    )(tab, wt, kt, x, prv, nxt)


def depth_matrix(wt, q, transpose):
    n = q // QF
    f = q % QF
    i = lax.broadcasted_iota(jnp.int32, (128, 128), 0)
    j = lax.broadcasted_iota(jnp.int32, (128, 128), 1)
    off = (i - j if transpose else j - i) + (257 - n)
    off = jnp.bitwise_and(off, 127)
    w = jnp.zeros((128, 128), F32)
    for m in range(4):
        w = jnp.where(off == m, wt[f, m], w)
    return w


def depth_product(wt, q, transpose, r, k):
    w = depth_matrix(wt, q, transpose)
    pair = [r[:, 2 * k + h].reshape(128, 128) for h in range(2)]
    y = jnp.dot(w, jnp.concatenate(pair, axis=1), precision=lax.Precision.HIGHEST, preferred_element_type=F32)
    return y[:, :128], y[:, 128:]


def depth_kernel(code, wt, r, a, out):
    @pl.loop(0, BRICKS)
    def _(k):
        ys = depth_product(wt, code[k], False, r, k)
        for h in range(2):
            u = ys[h] + a[:, 2 * k + h].reshape(128, 128)
            tiles = pltpu.roll(u, 4, 0).reshape(PEERS, 8, 128)
            out[:, 0, 2 * k + h] = tiles
            out[:, 1, 2 * k + h] = jnp.concatenate([tiles[1:], tiles[:1]], axis=0)


def depth(code, wt, r, a):
    return pl.pallas_call(
        depth_kernel,
        in_specs=[SMEM, SMEM, VMEM, VMEM],
        out_specs=VMEM,
        out_shape=jax.ShapeDtypeStruct((PEERS, 2, RB, 8, 128), F32),
        compiler_params=params(),
        name="depth",
    )(code, wt, r, a)


def depth_adjoint_kernel(code, wt, r, out):
    @pl.loop(0, BRICKS)
    def _(k):
        ys = depth_product(wt, code[k], True, r, k)
        for h in range(2):
            out[:, 2 * k + h] = ys[h].reshape(PEERS, 8, 128)


def depth_adjoint(code, wt, r):
    return pl.pallas_call(
        depth_adjoint_kernel,
        in_specs=[SMEM, SMEM, VMEM],
        out_specs=VMEM,
        out_shape=turned_shape(),
        compiler_params=params(),
        name="depth_adjoint",
    )(code, wt, r)


def to_next(x, axis, count):
    return lax.ppermute(x, axis, [(i, (i + 1) % count) for i in range(count)])


def to_prev(x, axis, count):
    return lax.ppermute(x, axis, [((i + 1) % count, i) for i in range(count)])


def swap(x):
    return lax.all_to_all(x, "gy", split_axis=0, concat_axis=0, tiled=True)


def body(velocity, states, pull_plan, send_plan, codes):
    gx = lax.axis_size("gx")
    gy = lax.axis_size("gy")
    top = to_next(states[:, -1], "gx", gx)
    bottom = to_prev(states[:, 0], "gx", gx)
    left = to_next(states[:, :, -1], "gy", gy)
    right = to_prev(states[:, :, 0], "gy", gy)
    state_args = (states, top, bottom, left, right)
    wt = jnp.asarray(WEIGHTS, F32)
    kt = jnp.asarray(PAIRS, F32)
    code = codes[2].reshape(BRICKS)
    mine = jnp.concatenate(
        [send_plan.reshape(32), pull_plan.reshape(BRICKS), codes.reshape(3 * BRICKS), jnp.zeros((72,), jnp.int32)]
    )
    tab = swap(jnp.broadcast_to(mine, (PEERS, 128)))

    a0 = source(0, velocity, state_args)
    a1 = source(1, velocity, state_args)
    x = swap(a0)
    o = pull(tab, wt, x, to_next(x[:, RB - 1], "gx", gx), to_prev(x[:, 0], "gx", gx))
    u = swap(depth(code, wt, swap(o), a1))
    y, lo, hi = normal(tab, wt, kt, u, to_next(u[:, :, RB - 1], "gx", gx), to_prev(u[:, :, 0], "gx", gx))
    y = y.at[:, RB - 1].add(to_prev(lo, "gx", gx)).at[:, 0].add(to_next(hi, "gx", gx))
    adj1 = swap(y)
    v = swap(depth_adjoint(code, wt, adj1))
    y, lo, hi = push(tab, wt, v)
    y = y.at[:, RB - 1].add(to_prev(lo, "gx", gx)).at[:, 0].add(to_next(hi, "gx", gx))
    adj0 = swap(y)
    return force(adj1, adj0, state_args)


def solution(mesh):
    return jax.shard_map(
        body,
        mesh=mesh,
        in_specs=(
            P(None, "gx", "gy", None),
            P(None, "gx", "gy", None),
            P("gx", "gy"),
            P("gx", "gy", None, None),
            P(None, "gx", "gy"),
        ),
        out_specs=P(None, "gx", "gy", None),
        check_vma=False,
    )
```

```python
import functools

import jax
import jax.numpy as jnp
import numpy as np
from jax import lax
from jax.experimental import pallas as pl
from jax.experimental.pallas import tpu as pltpu
from jax.sharding import PartitionSpec as P

QF = 8
PEERS = 16
RB = 12
BRICKS = 6


def weights_of(f):
    return np.array(
        [
            -f * (f - 1.0) * (f - 2.0) / 6.0,
            (f + 1.0) * (f - 1.0) * (f - 2.0) / 2.0,
            -(f + 1.0) * f * (f - 2.0) / 2.0,
            (f + 1.0) * f * (f - 1.0) / 6.0,
        ]
    )


WEIGHTS = np.stack([weights_of(k / QF) for k in range(QF)])
PAIRS = np.stack([[np.dot(w[: 4 - d], w[d:]) for d in range(4)] for w in WEIGHTS])

VMEM = pl.BlockSpec(memory_space=pltpu.VMEM)
SMEM = pl.BlockSpec(memory_space=pltpu.SMEM)
F32 = jnp.float32


def params(mib=48):
    return pltpu.CompilerParams(vmem_limit_bytes=mib * 1024 * 1024)


def turned_shape(blocks=RB):
    return jax.ShapeDtypeStruct((PEERS, blocks, 8, 128), F32)


def gradients(st, top, bottom, left, right, rb, k):
    rows = pl.ds(rb * 8, 8)
    x = st[k, rows]
    before = st[k, jnp.maximum(rb * 8 - 1, 0)]
    before = jnp.where(rb == 0, jnp.zeros_like(before) if top is None else top[...], before)
    after = st[k, jnp.minimum(rb * 8 + 8, 95)]
    after = jnp.where(rb == RB - 1, jnp.zeros_like(after) if bottom is None else bottom[...], after)
    up = jnp.concatenate([x[1:], after[None]], axis=0)
    down = jnp.concatenate([before[None], x[:-1]], axis=0)
    col = lax.broadcasted_iota(jnp.int32, x.shape, 1)
    lo = 0.0 if left is None else left[0, rows][:, None, :]
    hi = 0.0 if right is None else right[0, rows][:, None, :]
    nxt = jnp.where(col == 15, hi, pltpu.roll(x, 15, 1))
    prv = jnp.where(col == 0, lo, pltpu.roll(x, 1, 1))
    return (
        (up - down) * 0.5,
        (nxt - prv) * 0.5,
        (pltpu.roll(x, 127, 2) - pltpu.roll(x, 1, 2)) * 0.5,
    )


def turn(x):
    return x.reshape(128, 128).T.reshape(PEERS, 8, 128)


def contract(v, g):
    return -0.5 * (v[0] * g[0] + v[1] * g[1] + v[2] * g[2])


def pre_kernel(v, st, out, sides, to_prv, to_nxt):
    i = pl.program_id(0)
    for j in range(3):
        rb = 3 * i + j
        vb = v[:, 8 * j : 8 * j + 8]
        a = contract(vb, gradients(st, None, None, None, None, rb, 0))
        out[:, j] = turn(a)
        rows = pl.ds(rb * 8, 8)
        sides[0, rows] = 0.25 * vb[1, :, 0]
        sides[1, rows] = -0.25 * vb[1, :, 15]
        if j == 0:

            @pl.when(i == 0)
            def _():
                to_prv[0] = a[0]
                to_prv[1] = vb[0, 0]
                to_prv[2] = a[1]
                to_prv[3] = st[0, 0]

        if j == 2:

            @pl.when(i == RB // 3 - 1)
            def _():
                to_nxt[0] = a[7]
                to_nxt[1] = vb[0, 7]
                to_nxt[2] = st[0, 95]


def pre(velocity, states):
    return pl.pallas_call(
        pre_kernel,
        grid=(RB // 3,),
        in_specs=[pl.BlockSpec((3, 24, 16, 128), lambda i: (0, i, 0, 0)), state_spec(0)],
        out_specs=[
            pl.BlockSpec((PEERS, 3, 8, 128), lambda i: (0, i, 0, 0)),
            whole((2, 96, 128)),
            whole((4, 16, 128)),
            whole((3, 16, 128)),
        ],
        out_shape=[
            turned_shape(RB + 1),
            jax.ShapeDtypeStruct((2, 96, 128), F32),
            jax.ShapeDtypeStruct((4, 16, 128), F32),
            jax.ShapeDtypeStruct((3, 16, 128), F32),
        ],
        compiler_params=params(16),
        cost_estimate=COST,
        name="pre",
    )(velocity, states)


def rims_kernel(prv, nxt, sides, left, right, ends, to_prv, to_nxt):
    col = lax.broadcasted_iota(jnp.int32, (16, 128), 0)

    def side(row):
        lo = sides[0, row : row + 1] * left[0, row : row + 1]
        hi = sides[1, row : row + 1] * right[0, row : row + 1]
        return jnp.where(col == 0, lo, 0.0) + jnp.where(col == 15, hi, 0.0)

    to_prv[0] = prv[0] + side(0)
    to_prv[1] = prv[1]
    to_prv[2] = prv[2] + side(1)
    to_prv[3] = prv[3]
    to_prv[4] = ends[0]
    to_nxt[0] = nxt[0] + side(95)
    to_nxt[1] = nxt[1]
    to_nxt[2] = nxt[2]
    to_nxt[3] = ends[1]


def rims(prv, nxt, sides, left, right, ends):
    return pl.pallas_call(
        rims_kernel,
        in_specs=[VMEM] * 6,
        out_specs=[VMEM, VMEM],
        out_shape=[jax.ShapeDtypeStruct((5, 16, 128), F32), jax.ShapeDtypeStruct((4, 16, 128), F32)],
        compiler_params=params(16),
        name="rims",
    )(prv, nxt, sides, left, right, ends)


def columns_kernel(a, sides, left, right, out):
    col = lax.broadcasted_iota(jnp.int32, (8, 16, 128), 1)
    for j in range(3):
        rows = pl.ds(8 * j, 8)
        lo = (sides[0, rows] * left[0, rows])[:, None, :]
        hi = (sides[1, rows] * right[0, rows])[:, None, :]
        out[:, j] = a[:, j] + turn(jnp.where(col == 0, lo, 0.0) + jnp.where(col == 15, hi, 0.0))


def columns(a, sides, left, right):
    block = pl.BlockSpec((PEERS, 3, 8, 128), lambda i: (0, i, 0, 0))
    side = pl.BlockSpec((1, 24, 128), lambda i: (0, i, 0))
    return pl.pallas_call(
        columns_kernel,
        grid=(RB // 3,),
        in_specs=[block, pl.BlockSpec((2, 24, 128), lambda i: (0, i, 0)), side, side],
        out_specs=block,
        out_shape=turned_shape(RB + 1),
        input_output_aliases={0: 0},
        compiler_params=params(16),
        cost_estimate=COST,
        name="columns",
    )(a, sides, left, right)


def source1_kernel(v, st, top, bottom, left, right, out):
    g = gradients(st, top, bottom, left, right, pl.program_id(0), 0)
    out[:, 0] = turn(contract(v, g))


def whole(shape):
    return pl.BlockSpec(shape, lambda i: (0,) * len(shape))


def state_spec(k):
    return pl.BlockSpec((1, 96, 16, 128), lambda i: (k, 0, 0, 0))


def edge_specs(k):
    side = pl.BlockSpec((1, 96, 128), lambda i: (k, 0, 0))
    return [whole((16, 128)), whole((16, 128)), side, side]


def natural3(f):
    return pl.BlockSpec((3, 8, 16, 128), lambda i: (0, f(i), 0, 0))


def turned(f):
    return pl.BlockSpec((PEERS, 1, 8, 128), lambda i: (0, f(i), 0, 0))


def same(i):
    return i


COST = pl.CostEstimate(flops=20_000_000, bytes_accessed=6_000_000, transcendentals=0)


def source1(velocity, states, edges):
    return pl.pallas_call(
        source1_kernel,
        grid=(RB,),
        in_specs=[natural3(same), state_spec(1)] + edge_specs(1),
        out_specs=turned(same),
        out_shape=turned_shape(RB),
        compiler_params=params(16),
        cost_estimate=COST,
        name="source1",
    )(velocity, states, *edges)


def close_kernel(a, my_prv, my_nxt, from_nxt, from_prv, table, out):
    i = pl.program_id(0)
    row = lax.broadcasted_iota(jnp.int32, (8, 16, 128), 0)
    zero = jnp.zeros((8, 16, 128), F32)
    lane = lax.broadcasted_iota(jnp.int32, (PEERS, 8, 128), 2)

    @pl.when(i == 0)
    def _():
        x = 0.25 * my_prv[1] * from_prv[2]
        out[:, 0] = a[:, 0] + turn(jnp.where(row == 0, x[None], zero))

    @pl.when(i == 1)
    def _():
        x = -0.25 * my_nxt[1] * from_nxt[3]
        out[:, 0] = a[:, 0] + turn(jnp.where(row == 7, x[None], zero))

    @pl.when(i == 2)
    def _():
        before = from_prv[0] - 0.25 * from_prv[1] * my_prv[3]
        after = from_nxt[0] + 0.25 * from_nxt[1] * my_nxt[2]
        x = jnp.where(row == 7, before[None], zero)
        x = jnp.where(row == 0, after[None], x)
        x = jnp.where(row == 1, from_nxt[2][None], x)
        inner = (lane >= 32) & (lane < 112)
        out[:, 0] = jnp.where(inner, table[...][None], turn(x))


def close(a, my_prv, my_nxt, from_nxt, from_prv, table):
    def block(i):
        return jnp.minimum(i * (RB - 1), RB)

    return pl.pallas_call(
        close_kernel,
        grid=(3,),
        in_specs=[
            turned(block),
            whole((5, 16, 128)),
            whole((4, 16, 128)),
            whole((5, 16, 128)),
            whole((4, 16, 128)),
            whole((1, 128)),
        ],
        out_specs=turned(block),
        out_shape=turned_shape(RB + 1),
        input_output_aliases={0: 0},
        compiler_params=params(16),
        name="close",
    )(a, my_prv, my_nxt, from_nxt, from_prv, table)


def force_block(adj1, adj0, s1, e1, s0, e0, rb, out):
    b1 = (adj1.reshape(128, 128).T * -0.5).reshape(8, 16, 128)
    b0 = (adj0.reshape(128, 128).T * -0.5).reshape(8, 16, 128)
    g1 = gradients(s1, *e1, rb, 0)
    g0 = gradients(s0, *e0, rb, 0)
    for c in range(3):
        out[c] = b1 * g1[c] + b0 * g0[c]


def force_kernel(adj1, adj0, s1, t1, b1, l1, r1, s0, t0, b0, l0, r0, out):
    rb = pl.program_id(0) + 1
    force_block(adj1[:, 0], adj0[:, 0], s1, (t1, b1, l1, r1), s0, (t0, b0, l0, r0), rb, out)


def force_edge_kernel(adj1, adj0, s1, t1, b1, l1, r1, s0, t0, b0, l0, r0, from_nxt, from_prv, prior, out):
    i = pl.program_id(0)
    lane = lax.broadcasted_iota(jnp.int32, (PEERS, 8, 128), 2)
    x = jnp.where((i == 0) & (lane < 32), from_prv[...], 0.0)
    x = x + jnp.where((i == 1) & (lane >= 112), from_nxt[...], 0.0)
    force_block(adj1[:, 0], adj0[:, 0] + x, s1, (t1, b1, l1, r1), s0, (t0, b0, l0, r0), i * (RB - 1), out)


def force(adj1, adj0, states, e1, e0):
    def specs(f):
        return [turned(f), turned(f), state_spec(1)] + edge_specs(1) + [state_spec(0)] + edge_specs(0)

    shape = jax.ShapeDtypeStruct((3, 96, 16, 128), F32)
    rim = adj0[:, RB]
    from_nxt = to_prev(rim, "gx", lax.axis_size("gx"))
    from_prv = to_next(rim, "gx", lax.axis_size("gx"))
    args = (adj1, adj0, states, *e1, states, *e0)

    def inner(i):
        return i + 1

    def outer(i):
        return i * (RB - 1)

    main = pl.pallas_call(
        force_kernel,
        grid=(RB - 2,),
        in_specs=specs(inner),
        out_specs=natural3(inner),
        out_shape=shape,
        compiler_params=params(24),
        cost_estimate=COST,
        name="force",
    )(*args)
    return pl.pallas_call(
        force_edge_kernel,
        grid=(2,),
        in_specs=specs(outer) + [whole((PEERS, 8, 128)), whole((PEERS, 8, 128)), pl.BlockSpec(memory_space=pl.ANY)],
        out_specs=natural3(outer),
        out_shape=shape,
        input_output_aliases={14: 0},
        compiler_params=params(24),
        name="force_edge",
    )(*args, from_nxt, from_prv, main)


def lanes():
    return lax.broadcasted_iota(jnp.int32, (8, 128), 1)


def column_taps(x):
    col = lax.broadcasted_iota(jnp.int32, x.shape, 2) % 16
    up = pltpu.roll(x, 16, 2)
    dn = pltpu.roll(x, 112, 2)
    after = jnp.concatenate([up[1:], up[:1]], axis=0)
    before = jnp.concatenate([dn[-1:], dn[:-1]], axis=0)
    return (
        pltpu.roll(jnp.where(col == 15, before, x), 1, 2),
        x,
        pltpu.roll(jnp.where(col == 0, after, x), 127, 2),
        pltpu.roll(jnp.where(col < 2, after, x), 126, 2),
    )


def column_taps_adjoint(t0, t1, t2, t3):
    col = lax.broadcasted_iota(jnp.int32, t1.shape, 2) % 16
    p0 = pltpu.roll(t0, 127, 2)
    p2 = pltpu.roll(t2, 1, 2)
    p3 = pltpu.roll(t3, 2, 2)
    own = t1 + jnp.where(col == 15, 0.0, p0) + jnp.where(col == 0, 0.0, p2) + jnp.where(col < 2, 0.0, p3)
    after = jnp.where(col == 0, p2, 0.0) + jnp.where(col < 2, p3, 0.0)
    before = jnp.where(col == 15, p0, 0.0)
    after = pltpu.roll(after, 112, 2)
    before = pltpu.roll(before, 16, 2)
    after = jnp.concatenate([after[-1:], after[:-1]], axis=0)
    before = jnp.concatenate([before[1:], before[:1]], axis=0)
    return own + after + before


def fill_taps(taps, e, x):
    for t, y in enumerate(column_taps(x)):
        taps[t, pl.ds(e * PEERS, PEERS)] = y


def fill_all(taps, x):
    @pl.loop(0, RB // 3)
    def _(i):
        for j in range(3):
            fill_taps(taps, 3 * i + j + 1, x(3 * i + j))

    for t, y in enumerate(column_taps(x(RB))):
        taps[t, pl.ds(0, PEERS)] = y
        taps[t, pl.ds((RB + 1) * PEERS, PEERS)] = y


def fill_weights(wv, values):
    for f in range(QF):
        for t in range(4):
            wv[f, t] = jnp.full((8, 128), float(values[f, t]), F32)


def brick_plan(tab, wv, b):
    base = tab[0, b]
    u = tab[1, b]
    v = tab[2, b]
    return base, [wv[u, t] for t in range(4)], [wv[v, t] for t in range(4)]


def brick_forward(taps, base, wr, wc):
    lane = lanes()
    c = []
    for i in range(4):
        acc = [wc[t] * taps[t, base + i * PEERS] for t in range(4)]
        c.append((acc[0] + acc[1]) + (acc[2] + acc[3]))
    outs = []
    for h in range(2):
        prv, cur, nxt = c[h], c[h + 1], c[h + 2]
        outs.append(
            (wr[0] * pltpu.roll(jnp.where(lane >= 112, prv, cur), 16, 1) + wr[1] * cur)
            + (
                wr[2] * pltpu.roll(jnp.where(lane < 16, nxt, cur), 112, 1)
                + wr[3] * pltpu.roll(jnp.where(lane < 32, nxt, cur), 96, 1)
            )
        )
    return outs


def brick_rows_adjoint(wr, v):
    lane = lanes()
    lo, own, hi = [], [], []
    for h in range(2):
        p0 = wr[0] * pltpu.roll(v[h], 112, 1)
        p2 = wr[2] * pltpu.roll(v[h], 16, 1)
        p3 = wr[3] * pltpu.roll(v[h], 32, 1)
        lo.append(jnp.where(lane >= 112, p0, 0.0))
        own.append(
            (wr[1] * v[h] + jnp.where(lane >= 112, 0.0, p0))
            + (jnp.where(lane < 16, 0.0, p2) + jnp.where(lane < 32, 0.0, p3))
        )
        hi.append(jnp.where(lane < 16, p2, 0.0) + jnp.where(lane < 32, p3, 0.0))
    return [lo[0], own[0] + lo[1], own[1] + hi[0], hi[1]]


def brick_add(acc, base, wc, c):
    for i in range(4):
        for t in range(4):
            acc[t, base + i * PEERS] = acc[t, base + i * PEERS] + wc[t] * c[i]


def pull_kernel(tab, x, out, taps, wv):
    fill_weights(wv, WEIGHTS)
    fill_all(taps, lambda rb: x[:, rb])

    @pl.loop(0, PEERS)
    def _(d):
        plans = [brick_plan(tab, wv, d * BRICKS + k) for k in range(BRICKS)]
        for k in range(BRICKS):
            base, wr, wc = plans[k]
            o = brick_forward(taps, base, wr, wc)
            for h in range(2):
                out[d, 2 * k + h] = o[h]


TAPS = pltpu.VMEM((4, PEERS * (RB + 2), 8, 128), F32)
WV = pltpu.VMEM((QF, 4, 8, 128), F32)


def pull(tab, x):
    return pl.pallas_call(
        pull_kernel,
        in_specs=[SMEM, VMEM],
        out_specs=VMEM,
        out_shape=turned_shape(),
        scratch_shapes=[TAPS, WV],
        compiler_params=params(24),
        name="pull",
    )(tab, x)


def clear(acc):
    @pl.loop(0, RB + 2)
    def _(e):
        acc[:, pl.ds(e * PEERS, PEERS)] = jnp.zeros((4, PEERS, 8, 128), F32)


def gather_taps(acc, e):
    return column_taps_adjoint(*[acc[t, pl.ds(e * PEERS, PEERS)] for t in range(4)])


def spill_inner(acc, out):
    @pl.loop(0, RB // 3)
    def _(i):
        for j in range(3):
            out[:, 3 * i + j] = gather_taps(acc, 3 * i + j + 1)


def push_kernel(tab, v, out, acc, wv):
    fill_weights(wv, WEIGHTS)
    clear(acc)

    @pl.loop(0, PEERS)
    def _(d):
        plans = [brick_plan(tab, wv, d * BRICKS + k) for k in range(BRICKS)]
        cs = [brick_rows_adjoint(plans[k][1], [v[d, 2 * k], v[d, 2 * k + 1]]) for k in range(BRICKS)]
        for k in range(BRICKS):
            brick_add(acc, plans[k][0], plans[k][2], cs[k])

    spill_inner(acc, out)
    out[:, RB] = gather_taps(acc, 0) + gather_taps(acc, RB + 1)


def push(tab, v):
    return pl.pallas_call(
        push_kernel,
        in_specs=[SMEM, VMEM],
        out_specs=VMEM,
        out_shape=turned_shape(RB + 1),
        scratch_shapes=[TAPS, WV],
        compiler_params=params(24),
        name="push",
    )(tab, v)


def normal_kernel(tab, x, prv, nxt, out, lo, hi, taps, acc, wv, kv):
    fill_weights(wv, WEIGHTS)
    fill_weights(kv, PAIRS)
    clear(acc)
    for q in range(2):
        fill_taps(taps.at[q], 0, prv[:, q])
        fill_taps(taps.at[q], RB + 1, nxt[:, q])

        @pl.loop(0, RB // 2)
        def _(i):
            for j in range(2):
                fill_taps(taps.at[q], 2 * i + j + 1, x[:, q, 2 * i + j])

    @pl.loop(0, PEERS)
    def _(d):
        sub = lax.broadcasted_iota(jnp.int32, (8, 128), 0)
        plans = [brick_plan(tab, wv, d * BRICKS + k) for k in range(BRICKS)]
        cs = []
        for k in range(BRICKS):
            base, wr, wc = plans[k]
            f = tab[3, d * BRICKS + k]
            kw = [kv[f, t] for t in range(4)]
            t0 = brick_forward(taps.at[0], base, wr, wc)
            t1 = brick_forward(taps.at[1], base, wr, wc)
            v = []
            for h in range(2):

                def plane(a):
                    return pltpu.roll(jnp.where(sub >= a, t0[h], t1[h]), 8 - a, 0)

                terms = [kw[0] * plane(4)]
                for dd in range(1, 4):
                    terms.append(kw[dd] * (plane(4 - dd) + plane(4 + dd)))
                v.append((terms[0] + terms[1]) + (terms[2] + terms[3]))
            cs.append(brick_rows_adjoint(wr, v))
        for k in range(BRICKS):
            brick_add(acc, plans[k][0], plans[k][2], cs[k])

    lo[...] = gather_taps(acc, 0)
    hi[...] = gather_taps(acc, RB + 1)
    spill_inner(acc, out)


EDGE = jax.ShapeDtypeStruct((PEERS, 8, 128), F32)


def normal(tab, x, prv, nxt):
    return pl.pallas_call(
        normal_kernel,
        in_specs=[SMEM, VMEM, VMEM, VMEM],
        out_specs=[VMEM, VMEM, VMEM],
        out_shape=[turned_shape(), EDGE, EDGE],
        scratch_shapes=[pltpu.VMEM((2, 4, PEERS * (RB + 2), 8, 128), F32), TAPS, WV, WV],
        compiler_params=params(32),
        name="normal",
    )(tab, x, prv, nxt)


def depth_matrix(wt, q, transpose):
    n = q // QF
    f = q % QF
    i = lax.broadcasted_iota(jnp.int32, (128, 128), 0)
    j = lax.broadcasted_iota(jnp.int32, (128, 128), 1)
    off = (i - j if transpose else j - i) + (257 - n)
    off = jnp.bitwise_and(off, 127)
    w = jnp.zeros((128, 128), F32)
    for m in range(4):
        w = jnp.where(off == m, wt[f, m], w)
    return w


def depth_product(wt, q, transpose, r, k):
    w = depth_matrix(wt, q, transpose)
    pair = [r[:, 2 * k + h].reshape(128, 128) for h in range(2)]
    y = jnp.dot(w, jnp.concatenate(pair, axis=1), precision=lax.Precision.HIGHEST, preferred_element_type=F32)
    return y[:, :128], y[:, 128:]


def depth_kernel(code, wt, r, a, out):
    @pl.loop(0, BRICKS)
    def _(k):
        ys = depth_product(wt, code[k], False, r, k)
        for h in range(2):
            u = ys[h] + a[:, 2 * k + h].reshape(128, 128)
            tiles = pltpu.roll(u, 4, 0).reshape(PEERS, 8, 128)
            out[:, 0, 2 * k + h] = tiles
            out[:, 1, 2 * k + h] = jnp.concatenate([tiles[1:], tiles[:1]], axis=0)


def depth(code, wt, r, a):
    return pl.pallas_call(
        depth_kernel,
        in_specs=[SMEM, SMEM, VMEM, VMEM],
        out_specs=VMEM,
        out_shape=jax.ShapeDtypeStruct((PEERS, 2, RB, 8, 128), F32),
        compiler_params=params(24),
        name="depth",
    )(code, wt, r, a)


def depth_adjoint_kernel(code, wt, r, out):
    @pl.loop(0, BRICKS)
    def _(k):
        ys = depth_product(wt, code[k], True, r, k)
        for h in range(2):
            out[:, 2 * k + h] = ys[h].reshape(PEERS, 8, 128)


def depth_adjoint(code, wt, r):
    return pl.pallas_call(
        depth_adjoint_kernel,
        in_specs=[SMEM, SMEM, VMEM],
        out_specs=VMEM,
        out_shape=turned_shape(),
        compiler_params=params(24),
        name="depth_adjoint",
    )(code, wt, r)


def to_next(x, axis, count):
    return lax.ppermute(x, axis, [(i, (i + 1) % count) for i in range(count)])


def to_prev(x, axis, count):
    return lax.ppermute(x, axis, [((i + 1) % count, i) for i in range(count)])


def swap(x):
    return lax.all_to_all(x, "gy", split_axis=0, concat_axis=0, tiled=True)


def brick_table(raw):
    t = raw.astype(jnp.int32)
    slot = t[:, 32:38]
    sends = t[:, :32].reshape(PEERS, PEERS, 2).transpose(1, 0, 2).reshape(PEERS, 1, 32)
    hit = slot[:, :, None] == jnp.arange(32)[None, None, :]
    local = jnp.sum(jnp.where(hit, sends, 0), axis=2)
    rows = [2 * PEERS * local + slot // 2, t[:, 38:44], t[:, 44:50], t[:, 50:56] % QF]
    return jnp.stack(rows).reshape(4, PEERS * BRICKS)


def body(velocity, states, pull_plan, send_plan, codes):
    gx = lax.axis_size("gx")
    gy = lax.axis_size("gy")
    left = to_next(states[:, :, -1], "gy", gy)
    right = to_prev(states[:, :, 0], "gy", gy)
    ends = jnp.stack([states[1, 0], states[1, -1]])
    a0, sides, my_prv, my_nxt = pre(velocity, states)
    wt = jnp.asarray(WEIGHTS, F32)
    code = codes[2].reshape(BRICKS)
    mine = [send_plan.reshape(32), pull_plan.reshape(BRICKS), codes.reshape(3 * BRICKS)]
    table = jnp.concatenate([jnp.zeros((32,), jnp.int32)] + mine + [jnp.zeros((40,), jnp.int32)])
    table = table.astype(F32).reshape(1, 128)

    my_prv, my_nxt = rims(my_prv, my_nxt, sides, left, right, ends)
    from_nxt = to_prev(my_prv, "gx", gx)
    from_prv = to_next(my_nxt, "gx", gx)
    a0 = close(columns(a0, sides, left, right), my_prv, my_nxt, from_nxt, from_prv, table)
    e0 = (from_prv[2], from_nxt[3], left, right)
    e1 = (from_prv[3], from_nxt[4], left, right)
    a1 = source1(velocity, states, e1)

    x = swap(a0)
    tab = brick_table(x[:, RB, 0, 32:88])
    r = swap(pull(tab, x))
    u = swap(depth(code, wt, r, a1))
    y, lo, hi = normal(tab, u, to_next(u[:, :, RB - 1], "gx", gx), to_prev(u[:, :, 0], "gx", gx))
    y = y.at[:, RB - 1].add(to_prev(lo, "gx", gx)).at[:, 0].add(to_next(hi, "gx", gx))
    adj1 = swap(y)
    v = swap(depth_adjoint(code, wt, adj1))
    adj0 = swap(push(tab, v))
    return force(adj1, adj0, states, e1, e0)


def solution(mesh):
    return jax.shard_map(
        body,
        mesh=mesh,
        in_specs=(
            P(None, "gx", "gy", None),
            P(None, "gx", "gy", None),
            P("gx", "gy"),
            P("gx", "gy", None, None),
            P(None, "gx", "gy"),
        ),
        out_specs=P(None, "gx", "gy", None),
        check_vma=False,
    )
```

```python
import functools

import jax
import jax.numpy as jnp
import numpy as np
from jax import lax
from jax.experimental import pallas as pl
from jax.experimental.pallas import tpu as pltpu
from jax.sharding import PartitionSpec as P

QF = 8
PEERS = 16
RB = 12
BRICKS = 6


def weights_of(f):
    return np.array(
        [
            -f * (f - 1.0) * (f - 2.0) / 6.0,
            (f + 1.0) * (f - 1.0) * (f - 2.0) / 2.0,
            -(f + 1.0) * f * (f - 2.0) / 2.0,
            (f + 1.0) * f * (f - 1.0) / 6.0,
        ]
    )


WEIGHTS = np.stack([weights_of(k / QF) for k in range(QF)])
PAIRS = np.stack([[np.dot(w[: 4 - d], w[d:]) for d in range(4)] for w in WEIGHTS])


def shift_matrix():
    m = np.zeros((2, 8, 16, 3, 8, 16), np.float32)
    for r in range(8):
        for j in range(16):
            for n, d in enumerate((-1, 1, 2)):
                inside = 0 <= j + d < 16
                m[0 if inside else 1, r, (j + d) % 16, n, r, j] = 1.0
    return m.reshape(256, 384)


SHIFT = shift_matrix()
BF16 = jnp.bfloat16

VMEM = pl.BlockSpec(memory_space=pltpu.VMEM)
SMEM = pl.BlockSpec(memory_space=pltpu.SMEM)
F32 = jnp.float32


def params(mib=48):
    return pltpu.CompilerParams(vmem_limit_bytes=mib * 1024 * 1024)


def turned_shape(blocks=RB):
    return jax.ShapeDtypeStruct((PEERS, blocks, 8, 128), F32)


def gradients(st, top, bottom, left, right, rb, k):
    rows = pl.ds(rb * 8, 8)
    x = st[k, rows]
    before = st[k, jnp.maximum(rb * 8 - 1, 0)]
    before = jnp.where(rb == 0, jnp.zeros_like(before) if top is None else top[2 + k], before)
    after = st[k, jnp.minimum(rb * 8 + 8, 95)]
    after = jnp.where(rb == RB - 1, jnp.zeros_like(after) if bottom is None else bottom[3 + k], after)
    up = jnp.concatenate([x[1:], after[None]], axis=0)
    down = jnp.concatenate([before[None], x[:-1]], axis=0)
    col = lax.broadcasted_iota(jnp.int32, x.shape, 1)
    lo = 0.0 if left is None else left[k, rows][:, None, :]
    hi = 0.0 if right is None else right[k, rows][:, None, :]
    nxt = jnp.where(col == 15, hi, pltpu.roll(x, 15, 1))
    prv = jnp.where(col == 0, lo, pltpu.roll(x, 1, 1))
    return (
        (up - down) * 0.5,
        (nxt - prv) * 0.5,
        (pltpu.roll(x, 127, 2) - pltpu.roll(x, 1, 2)) * 0.5,
    )


def turn(x):
    return x.reshape(128, 128).T.reshape(PEERS, 8, 128)


def contract(v, g):
    return -0.5 * (v[0] * g[0] + v[1] * g[1] + v[2] * g[2])


CHUNKS = 4


def pre_kernel(v_hbm, st_hbm, out0, out1, sides, to_prv, to_nxt, v, st, sems):
    rows = 96 // CHUNKS
    copies = [pltpu.make_async_copy(st_hbm.at[k], st.at[k], sems.at[k]) for k in range(2)]
    for i in range(CHUNKS):
        part = pl.ds(i * rows, rows)
        copies.append(pltpu.make_async_copy(v_hbm.at[:, part], v.at[:, part], sems.at[2 + i]))
    for c in copies:
        c.start()
    copies[0].wait()
    copies[1].wait()
    for i in range(CHUNKS):
        copies[2 + i].wait()

        @pl.loop(i * RB // CHUNKS, (i + 1) * RB // CHUNKS)
        def _(rb):
            block = pl.ds(rb * 8, 8)
            vb = v[:, block]
            a = contract(vb, gradients(st, None, None, None, None, rb, 0))
            out0[:, rb] = turn(a)
            out1[:, rb] = turn(contract(vb, gradients(st, None, None, None, None, rb, 1)))
            sides[0, block] = 0.25 * vb[1, :, 0]
            sides[1, block] = -0.25 * vb[1, :, 15]

            @pl.when(rb == 0)
            def _():
                to_prv[0] = a[0]
                to_prv[2] = a[1]

            @pl.when(rb == RB - 1)
            def _():
                to_nxt[0] = a[7]

    to_prv[1] = v[0, 0]
    to_prv[3] = st[0, 0]
    to_prv[4] = st[1, 0]
    to_nxt[1] = v[0, 95]
    to_nxt[2] = st[0, 95]
    to_nxt[3] = st[1, 95]


def in_hbm(x):
    return pltpu.with_memory_space_constraint(x, pltpu.HBM)


def pre(velocity, states):
    hbm = pl.BlockSpec(memory_space=pltpu.HBM)
    return pl.pallas_call(
        pre_kernel,
        in_specs=[hbm, hbm],
        out_specs=[VMEM] * 5,
        out_shape=[
            turned_shape(RB + 1),
            turned_shape(),
            jax.ShapeDtypeStruct((2, 96, 128), F32),
            jax.ShapeDtypeStruct((5, 16, 128), F32),
            jax.ShapeDtypeStruct((4, 16, 128), F32),
        ],
        scratch_shapes=[
            pltpu.VMEM((3, 96, 16, 128), F32),
            pltpu.VMEM((2, 96, 16, 128), F32),
            pltpu.SemaphoreType.DMA((2 + CHUNKS,)),
        ],
        compiler_params=params(24),
        cost_estimate=COST,
        name="pre",
    )(in_hbm(velocity), in_hbm(states))


def rims_kernel(prv, nxt, sides, left, right, to_prv, to_nxt):
    col = lax.broadcasted_iota(jnp.int32, (16, 128), 0)

    def side(row):
        lo = sides[0, row : row + 1] * left[0, row : row + 1]
        hi = sides[1, row : row + 1] * right[0, row : row + 1]
        return jnp.where(col == 0, lo, 0.0) + jnp.where(col == 15, hi, 0.0)

    to_prv[0] = prv[0] + side(0)
    to_prv[1] = prv[1]
    to_prv[2] = prv[2] + side(1)
    to_prv[3] = prv[3]
    to_prv[4] = prv[4]
    to_nxt[0] = nxt[0] + side(95)
    to_nxt[1] = nxt[1]
    to_nxt[2] = nxt[2]
    to_nxt[3] = nxt[3]


def rims(prv, nxt, sides, left, right):
    return pl.pallas_call(
        rims_kernel,
        in_specs=[VMEM] * 5,
        out_specs=[VMEM, VMEM],
        out_shape=[jax.ShapeDtypeStruct((5, 16, 128), F32), jax.ShapeDtypeStruct((4, 16, 128), F32)],
        compiler_params=params(16),
        name="rims",
    )(prv, nxt, sides, left, right)


def columns_kernel(a0, a1, sides, left, right, out0, out1):
    col = lax.broadcasted_iota(jnp.int32, (8, 16, 128), 1)
    for k, (a, out) in enumerate(((a0, out0), (a1, out1))):
        for j in range(3):
            rows = pl.ds(8 * j, 8)
            lo = (sides[0, rows] * left[k, rows])[:, None, :]
            hi = (sides[1, rows] * right[k, rows])[:, None, :]
            out[:, j] = a[:, j] + turn(jnp.where(col == 0, lo, 0.0) + jnp.where(col == 15, hi, 0.0))


def columns(a0, a1, sides, left, right):
    block = pl.BlockSpec((PEERS, 3, 8, 128), lambda i: (0, i, 0, 0))
    side = pl.BlockSpec((2, 24, 128), lambda i: (0, i, 0))
    return pl.pallas_call(
        columns_kernel,
        grid=(RB // 3,),
        in_specs=[block, block, side, side, side],
        out_specs=[block, block],
        out_shape=[turned_shape(RB + 1), turned_shape()],
        input_output_aliases={0: 0, 1: 1},
        compiler_params=params(16),
        cost_estimate=COST,
        name="columns",
    )(a0, a1, sides, left, right)


def whole(shape):
    return pl.BlockSpec(shape, lambda i: (0,) * len(shape))


def natural3(f):
    return pl.BlockSpec((3, 8, 16, 128), lambda i: (0, f(i), 0, 0))


def turned(f):
    return pl.BlockSpec((PEERS, 1, 8, 128), lambda i: (0, f(i), 0, 0))


def same(i):
    return i


COST = pl.CostEstimate(flops=20_000_000, bytes_accessed=6_000_000, transcendentals=0)


def close_kernel(a0, a1, my_prv, my_nxt, from_nxt, from_prv, table, out0, out1):
    i = pl.program_id(0)
    row = lax.broadcasted_iota(jnp.int32, (8, 16, 128), 0)
    zero = jnp.zeros((8, 16, 128), F32)
    lane = lax.broadcasted_iota(jnp.int32, (PEERS, 8, 128), 2)

    @pl.when(i == 0)
    def _():
        for k, (a, out) in enumerate(((a0, out0), (a1, out1))):
            x = 0.25 * my_prv[1] * from_prv[2 + k]
            out[:, 0] = a[:, 0] + turn(jnp.where(row == 0, x[None], zero))

    @pl.when(i == 1)
    def _():
        for k, (a, out) in enumerate(((a0, out0), (a1, out1))):
            x = -0.25 * my_nxt[1] * from_nxt[3 + k]
            out[:, 0] = a[:, 0] + turn(jnp.where(row == 7, x[None], zero))

    @pl.when(i == 2)
    def _():
        before = from_prv[0] - 0.25 * from_prv[1] * my_prv[3]
        after = from_nxt[0] + 0.25 * from_nxt[1] * my_nxt[2]
        x = jnp.where(row == 7, before[None], zero)
        x = jnp.where(row == 0, after[None], x)
        x = jnp.where(row == 1, from_nxt[2][None], x)
        inner = (lane >= 32) & (lane < 112)
        out0[:, 0] = jnp.where(inner, table[...][None], turn(x))


def close(a0, a1, my_prv, my_nxt, from_nxt, from_prv, table):
    def block(i):
        return jnp.minimum(i * (RB - 1), RB)

    def kept(i):
        return jnp.minimum(i * (RB - 1), RB - 1)

    return pl.pallas_call(
        close_kernel,
        grid=(3,),
        in_specs=[
            turned(block),
            turned(kept),
            whole((5, 16, 128)),
            whole((4, 16, 128)),
            whole((5, 16, 128)),
            whole((4, 16, 128)),
            whole((1, 128)),
        ],
        out_specs=[turned(block), turned(kept)],
        out_shape=[turned_shape(RB + 1), turned_shape()],
        input_output_aliases={0: 0, 1: 1},
        compiler_params=params(16),
        name="close",
    )(a0, a1, my_prv, my_nxt, from_nxt, from_prv, table)


def force_block(adj1, adj0, st, edges, rb, out):
    b1 = (adj1.reshape(128, 128).T * -0.5).reshape(8, 16, 128)
    b0 = (adj0.reshape(128, 128).T * -0.5).reshape(8, 16, 128)
    g1 = gradients(st, *edges, rb, 1)
    g0 = gradients(st, *edges, rb, 0)
    for c in range(3):
        out[c] = b1 * g1[c] + b0 * g0[c]


def force_kernel(adj1, adj0, st, top, bottom, left, right, out):
    force_block(adj1[:, 0], adj0[:, 0], st, (top, bottom, left, right), pl.program_id(0) + 1, out)


def force_edge_kernel(adj1, adj0, st, top, bottom, left, right, from_nxt, from_prv, prior, out):
    i = pl.program_id(0)
    lane = lax.broadcasted_iota(jnp.int32, (PEERS, 8, 128), 2)
    x = jnp.where((i == 0) & (lane < 32), from_prv[...], 0.0)
    x = x + jnp.where((i == 1) & (lane >= 112), from_nxt[...], 0.0)
    force_block(adj1[:, 0], adj0[:, 0] + x, st, (top, bottom, left, right), i * (RB - 1), out)


def force(adj1, adj0, states, edges):
    fixed = [whole((2, 96, 16, 128)), whole((4, 16, 128)), whole((5, 16, 128)), whole((2, 96, 128)), whole((2, 96, 128))]
    shape = jax.ShapeDtypeStruct((3, 96, 16, 128), F32)
    rim = adj0[:, RB]
    from_nxt = to_prev(rim, "gx", lax.axis_size("gx"))
    from_prv = to_next(rim, "gx", lax.axis_size("gx"))
    args = (adj1, adj0, states, *edges)

    def inner(i):
        return i + 1

    def outer(i):
        return i * (RB - 1)

    main = pl.pallas_call(
        force_kernel,
        grid=(RB - 2,),
        in_specs=[turned(inner), turned(inner)] + fixed,
        out_specs=natural3(inner),
        out_shape=shape,
        compiler_params=params(24),
        cost_estimate=COST,
        name="force",
    )(*args)
    return pl.pallas_call(
        force_edge_kernel,
        grid=(2,),
        in_specs=[turned(outer), turned(outer)]
        + fixed
        + [whole((PEERS, 8, 128)), whole((PEERS, 8, 128)), pl.BlockSpec(memory_space=pl.ANY)],
        out_specs=natural3(outer),
        out_shape=shape,
        input_output_aliases={9: 0},
        compiler_params=params(24),
        name="force_edge",
    )(*args, from_nxt, from_prv, main)


def lanes():
    return lax.broadcasted_iota(jnp.int32, (8, 128), 1)


def split(x):
    hi = x.astype(BF16)
    return hi, (x - hi.astype(F32)).astype(BF16)


def load_taps(lhs, taps, e, x):
    col = lax.broadcasted_iota(jnp.int32, x.shape, 2) % 16
    after = jnp.concatenate([x[1:], x[:1]], axis=0)
    before = jnp.concatenate([x[-1:], x[:-1]], axis=0)
    xh, xl = split(x.reshape(128, 128))
    eh, el = split(jnp.where(col < 2, after, before).reshape(128, 128))
    rows = pl.ds(e * 128, 128)
    lhs[rows, 0:128] = xh
    lhs[rows, 128:256] = eh
    lhs[rows, 256:384] = xl
    lhs[rows, 384:512] = el
    taps[1, pl.ds(e * PEERS, PEERS)] = x


def shift_taps(lhs, shift, taps, blocks):
    m = shift[...]
    y = jnp.dot(lhs[0 : blocks * 128, 0:512], jnp.concatenate([m, m], axis=0), preferred_element_type=F32)
    for n, t in enumerate((0, 2, 3)):
        taps[t, 0 : blocks * PEERS] = y[:, n * 128 : n * 128 + 128].reshape(blocks * PEERS, 8, 128)


def shift_taps_adjoint(lhs, shift_t, acc, put):
    @pl.loop(0, RB + 2)
    def _(e):
        rows = pl.ds(e * 128, 128)
        for n, t in enumerate((0, 2, 3)):
            h, l = split(acc[t, pl.ds(e * PEERS, PEERS)].reshape(128, 128))
            lhs[rows, n * 128 : n * 128 + 128] = h
            lhs[rows, 384 + n * 128 : 512 + n * 128] = l

    m = shift_t[...]
    y = jnp.dot(lhs[...], jnp.concatenate([m, m], axis=0), preferred_element_type=F32)
    col = lax.broadcasted_iota(jnp.int32, (PEERS, 8, 128), 2) % 16
    for e in range(RB + 2):
        own = y[e * 128 : e * 128 + 128, :128].reshape(PEERS, 8, 128)
        rim = y[e * 128 : e * 128 + 128, 128:].reshape(PEERS, 8, 128)
        after = jnp.concatenate([rim[-1:], rim[:-1]], axis=0)
        before = jnp.concatenate([rim[1:], rim[:1]], axis=0)
        put(e, acc[1, e * PEERS : (e + 1) * PEERS] + own + jnp.where(col < 2, after, before))


def fill_weights(wv, values):
    for f in range(QF):
        for t in range(4):
            wv[f, t] = jnp.full((8, 128), float(values[f, t]), F32)


def brick_plan(tab, wv, b):
    base = tab[0, b]
    u = tab[1, b]
    v = tab[2, b]
    return base, [wv[u, t] for t in range(4)], [wv[v, t] for t in range(4)]


def brick_columns(taps, base, wc):
    c = []
    for i in range(4):
        acc = [wc[t] * taps[t, base + i * PEERS] for t in range(4)]
        c.append((acc[0] + acc[1]) + (acc[2] + acc[3]))
    return c


def brick_rows(wr, c):
    lane = lanes()
    outs = []
    for h in range(2):
        prv, cur, nxt = c[h], c[h + 1], c[h + 2]
        outs.append(
            (wr[0] * pltpu.roll(jnp.where(lane >= 112, prv, cur), 16, 1) + wr[1] * cur)
            + (
                wr[2] * pltpu.roll(jnp.where(lane < 16, nxt, cur), 112, 1)
                + wr[3] * pltpu.roll(jnp.where(lane < 32, nxt, cur), 96, 1)
            )
        )
    return outs


def brick_rows_adjoint(wr, v):
    lane = lanes()
    lo, own, hi = [], [], []
    for h in range(2):
        p0 = wr[0] * pltpu.roll(v[h], 112, 1)
        p2 = wr[2] * pltpu.roll(v[h], 16, 1)
        p3 = wr[3] * pltpu.roll(v[h], 32, 1)
        lo.append(jnp.where(lane >= 112, p0, 0.0))
        own.append(
            (wr[1] * v[h] + jnp.where(lane >= 112, 0.0, p0))
            + (jnp.where(lane < 16, 0.0, p2) + jnp.where(lane < 32, 0.0, p3))
        )
        hi.append(jnp.where(lane < 16, p2, 0.0) + jnp.where(lane < 32, p3, 0.0))
    return [lo[0], own[0] + lo[1], own[1] + hi[0], hi[1]]


def brick_add(acc, base, wc, c):
    for i in range(4):
        for t in range(4):
            acc[t, base + i * PEERS] = acc[t, base + i * PEERS] + wc[t] * c[i]


BUF = pltpu.VMEM((BRICKS, 4, 8, 128), F32)


def each_peer(first, second, bufs):
    for k in range(BRICKS):
        first(0, k, bufs[0])

    @pl.loop(0, PEERS // 2)
    def _(i):
        d = 2 * i
        for k in range(BRICKS):
            second(d, k, bufs[0])
            first(d + 1, k, bufs[1])
        for k in range(BRICKS):
            second(d + 1, k, bufs[1])
            first(jnp.minimum(d + 2, PEERS - 1), k, bufs[0])


def pull_kernel(tab, shift, x, out, taps, wv, lhs, *bufs):
    fill_weights(wv, WEIGHTS)
    load_taps(lhs, taps, 0, x[:, RB])

    @pl.loop(0, RB)
    def _(rb):
        load_taps(lhs, taps, rb + 1, x[:, rb])

    shift_taps(lhs, shift, taps, RB + 1)
    for t in range(4):
        taps[t, (RB + 1) * PEERS :] = taps[t, 0:PEERS]

    def first(d, k, buf):
        base, _, wc = brick_plan(tab, wv, d * BRICKS + k)
        c = brick_columns(taps, base, wc)
        for i in range(4):
            buf[k, i] = c[i]

    def second(d, k, buf):
        _, wr, _ = brick_plan(tab, wv, d * BRICKS + k)
        o = brick_rows(wr, [buf[k, i] for i in range(4)])
        for h in range(2):
            out[d, 2 * k + h] = o[h]

    each_peer(first, second, bufs)


TAPS = pltpu.VMEM((4, PEERS * (RB + 2), 8, 128), F32)
WV = pltpu.VMEM((QF, 4, 8, 128), F32)


LHS = pltpu.VMEM(((RB + 2) * 128, 768), BF16)


def pull(tab, shift, x):
    return pl.pallas_call(
        pull_kernel,
        in_specs=[SMEM, VMEM, VMEM],
        out_specs=VMEM,
        out_shape=turned_shape(),
        scratch_shapes=[TAPS, WV, LHS, BUF, BUF],
        compiler_params=params(24),
        name="pull",
    )(tab, shift, x)


def clear(acc):
    @pl.loop(0, RB + 2)
    def _(e):
        acc[:, pl.ds(e * PEERS, PEERS)] = jnp.zeros((4, PEERS, 8, 128), F32)


def push_kernel(tab, shift_t, v, out, acc, wv, lhs, *bufs):
    fill_weights(wv, WEIGHTS)
    clear(acc)

    def first(d, k, buf):
        _, wr, _ = brick_plan(tab, wv, d * BRICKS + k)
        c = brick_rows_adjoint(wr, [v[d, 2 * k], v[d, 2 * k + 1]])
        for i in range(4):
            buf[k, i] = c[i]

    def second(d, k, buf):
        base, _, wc = brick_plan(tab, wv, d * BRICKS + k)
        brick_add(acc, base, wc, [buf[k, i] for i in range(4)])

    each_peer(first, second, bufs)

    def put(e, block):
        if e == 0:
            out[:, RB] = block
        elif e == RB + 1:
            out[:, RB] = out[:, RB] + block
        else:
            out[:, e - 1] = block

    shift_taps_adjoint(lhs, shift_t, acc, put)


def push(tab, shift_t, v):
    return pl.pallas_call(
        push_kernel,
        in_specs=[SMEM, VMEM, VMEM],
        out_specs=VMEM,
        out_shape=turned_shape(RB + 1),
        scratch_shapes=[TAPS, WV, LHS, BUF, BUF],
        compiler_params=params(24),
        name="push",
    )(tab, shift_t, v)


def normal_kernel(tab, shift, shift_t, x, prv, nxt, out, lo, hi, taps, acc, wv, kv, lhs, *bufs):
    fill_weights(wv, WEIGHTS)
    fill_weights(kv, PAIRS)
    clear(acc)
    for q in range(2):
        load_taps(lhs, taps.at[q], 0, prv[:, q])
        load_taps(lhs, taps.at[q], RB + 1, nxt[:, q])

        @pl.loop(0, RB)
        def _(rb):
            load_taps(lhs, taps.at[q], rb + 1, x[:, q, rb])

        shift_taps(lhs, shift, taps.at[q], RB + 2)

    def first(d, k, buf):
        sub = lax.broadcasted_iota(jnp.int32, (8, 128), 0)
        base, _, wc = brick_plan(tab, wv, d * BRICKS + k)
        c0 = brick_columns(taps.at[0], base, wc)
        c1 = brick_columns(taps.at[1], base, wc)
        f = tab[3, d * BRICKS + k]
        kw = [kv[f, t] for t in range(4)]
        for i in range(4):
            at = [pltpu.roll(jnp.where(sub >= a, c0[i], c1[i]), 8 - a, 0) for a in range(1, 8)]
            near = kw[0] * at[3] + kw[1] * (at[2] + at[4])
            buf[k, i] = near + (kw[2] * (at[1] + at[5]) + kw[3] * (at[0] + at[6]))

    def second(d, k, buf):
        base, wr, wc = brick_plan(tab, wv, d * BRICKS + k)
        c = brick_rows_adjoint(wr, brick_rows(wr, [buf[k, i] for i in range(4)]))
        brick_add(acc, base, wc, c)

    each_peer(first, second, bufs)

    def put(e, block):
        if e == 0:
            lo[...] = block
        elif e == RB + 1:
            hi[...] = block
        else:
            out[:, e - 1] = block

    shift_taps_adjoint(lhs, shift_t, acc, put)


EDGE = jax.ShapeDtypeStruct((PEERS, 8, 128), F32)


def normal(tab, shift, shift_t, x, prv, nxt):
    return pl.pallas_call(
        normal_kernel,
        in_specs=[SMEM, VMEM, VMEM, VMEM, VMEM, VMEM],
        out_specs=[VMEM, VMEM, VMEM],
        out_shape=[turned_shape(), EDGE, EDGE],
        scratch_shapes=[
            pltpu.VMEM((2, 4, PEERS * (RB + 2), 8, 128), F32),
            TAPS,
            WV,
            WV,
            LHS,
            BUF,
            BUF,
        ],
        compiler_params=params(24),
        name="normal",
    )(tab, shift, shift_t, x, prv, nxt)


def depth_matrix(q, transpose):
    n = q // QF
    f = (q % QF).astype(F32) * (1.0 / QF)
    weights = (
        f * (f - 1.0) * (f - 2.0) * (-1.0 / 6.0),
        (f + 1.0) * (f - 1.0) * (f - 2.0) * 0.5,
        (f + 1.0) * f * (f - 2.0) * -0.5,
        (f + 1.0) * f * (f - 1.0) * (1.0 / 6.0),
    )
    i = lax.broadcasted_iota(jnp.int32, (128, 128), 0)
    j = lax.broadcasted_iota(jnp.int32, (128, 128), 1)
    off = (i - j if transpose else j - i) + (257 - n)
    off = jnp.bitwise_and(off, 127)
    w = jnp.zeros((128, 128), F32)
    for m in range(4):
        w = jnp.where(off == m, weights[m], w)
    return w


def depth_product(q, transpose, r, k):
    wh, wl = split(depth_matrix(q, transpose))
    xh, xl = split(jnp.concatenate([r[:, 2 * k + h].reshape(128, 128) for h in range(2)], axis=1))
    y = jnp.dot(
        jnp.concatenate([wh, wl, wh], axis=1), jnp.concatenate([xh, xh, xl], axis=0), preferred_element_type=F32
    )
    return y[:, :128], y[:, 128:]


def depth_kernel(code, r, a, out):
    @pl.loop(0, BRICKS)
    def _(k):
        ys = depth_product(code[k], False, r, k)
        for h in range(2):
            u = ys[h] + a[:, 2 * k + h].reshape(128, 128)
            tiles = pltpu.roll(u, 4, 0).reshape(PEERS, 8, 128)
            out[:, 0, 2 * k + h] = tiles
            out[:, 1, 2 * k + h] = jnp.concatenate([tiles[1:], tiles[:1]], axis=0)


def depth(code, r, a):
    return pl.pallas_call(
        depth_kernel,
        in_specs=[SMEM, VMEM, VMEM],
        out_specs=VMEM,
        out_shape=jax.ShapeDtypeStruct((PEERS, 2, RB, 8, 128), F32),
        compiler_params=params(24),
        name="depth",
    )(code, r, a)


def depth_adjoint_kernel(code, r, out):
    @pl.loop(0, BRICKS)
    def _(k):
        ys = depth_product(code[k], True, r, k)
        for h in range(2):
            out[:, 2 * k + h] = ys[h].reshape(PEERS, 8, 128)


def depth_adjoint(code, r):
    return pl.pallas_call(
        depth_adjoint_kernel,
        in_specs=[SMEM, VMEM],
        out_specs=VMEM,
        out_shape=turned_shape(),
        compiler_params=params(24),
        name="depth_adjoint",
    )(code, r)


def to_next(x, axis, count):
    return lax.ppermute(x, axis, [(i, (i + 1) % count) for i in range(count)])


def to_prev(x, axis, count):
    return lax.ppermute(x, axis, [((i + 1) % count, i) for i in range(count)])


def swap(x):
    return lax.all_to_all(x, "gy", split_axis=0, concat_axis=0, tiled=True)


def brick_table(raw):
    t = raw.astype(jnp.int32)
    slot = t[:, 32:38]
    sends = t[:, :32].reshape(PEERS, PEERS, 2).transpose(1, 0, 2).reshape(PEERS, 1, 32)
    hit = slot[:, :, None] == jnp.arange(32)[None, None, :]
    local = jnp.sum(jnp.where(hit, sends, 0), axis=2)
    rows = [2 * PEERS * local + slot // 2, t[:, 38:44], t[:, 44:50], t[:, 50:56] % QF]
    return jnp.stack(rows).reshape(4, PEERS * BRICKS)


def body(velocity, states, pull_plan, send_plan, codes):
    gx = lax.axis_size("gx")
    gy = lax.axis_size("gy")
    left = to_next(states[:, :, -1], "gy", gy)
    right = to_prev(states[:, :, 0], "gy", gy)
    a0, a1, sides, my_prv, my_nxt = pre(velocity, states)
    shift = jnp.asarray(SHIFT, BF16)
    shift_t = jnp.asarray(SHIFT.T, BF16)
    code = codes[2].reshape(BRICKS)
    mine = [send_plan.reshape(32), pull_plan.reshape(BRICKS), codes.reshape(3 * BRICKS)]
    table = jnp.concatenate([jnp.zeros((32,), jnp.int32)] + mine + [jnp.zeros((40,), jnp.int32)])
    table = table.astype(F32).reshape(1, 128)

    my_prv, my_nxt = rims(my_prv, my_nxt, sides, left, right)
    from_nxt = to_prev(my_prv, "gx", gx)
    from_prv = to_next(my_nxt, "gx", gx)
    a0, a1 = columns(a0, a1, sides, left, right)
    a0, a1 = close(a0, a1, my_prv, my_nxt, from_nxt, from_prv, table)
    a0, code = lax.optimization_barrier((a0, code))
    x = swap(a0)
    tab = brick_table(x[:, RB, 0, 32:88])
    r = swap(pull(tab, shift, x))
    u = swap(depth(code, r, a1))
    y, lo, hi = normal(tab, shift, shift_t, u, to_next(u[:, :, RB - 1], "gx", gx), to_prev(u[:, :, 0], "gx", gx))
    y = y.at[:, RB - 1].add(to_prev(lo, "gx", gx)).at[:, 0].add(to_next(hi, "gx", gx))
    adj1 = swap(y)
    v = swap(depth_adjoint(code, adj1))
    adj0 = swap(push(tab, shift_t, v))
    return force(adj1, adj0, states, (from_prv, from_nxt, left, right))


def solution(mesh):
    return jax.shard_map(
        body,
        mesh=mesh,
        in_specs=(
            P(None, "gx", "gy", None),
            P(None, "gx", "gy", None),
            P("gx", "gy"),
            P("gx", "gy", None, None),
            P(None, "gx", "gy"),
        ),
        out_specs=P(None, "gx", "gy", None),
        check_vma=False,
    )
```

```python
import functools

import jax
import jax.numpy as jnp
import numpy as np
from jax import lax
from jax.experimental import pallas as pl
from jax.experimental.pallas import tpu as pltpu
from jax.sharding import PartitionSpec as P

QF = 8
PEERS = 16
RB = 12
BRICKS = 6


def weights_of(f):
    return np.array(
        [
            -f * (f - 1.0) * (f - 2.0) / 6.0,
            (f + 1.0) * (f - 1.0) * (f - 2.0) / 2.0,
            -(f + 1.0) * f * (f - 2.0) / 2.0,
            (f + 1.0) * f * (f - 1.0) / 6.0,
        ]
    )


WEIGHTS = np.stack([weights_of(k / QF) for k in range(QF)])
PAIRS = np.stack([[np.dot(w[: 4 - d], w[d:]) for d in range(4)] for w in WEIGHTS])


def shift_matrix():
    m = np.zeros((2, 8, 16, 3, 8, 16), np.float32)
    for r in range(8):
        for j in range(16):
            for n, d in enumerate((-1, 1, 2)):
                inside = 0 <= j + d < 16
                m[0 if inside else 1, r, (j + d) % 16, n, r, j] = 1.0
    return m.reshape(256, 384)


SHIFT = shift_matrix()
BF16 = jnp.bfloat16

VMEM = pl.BlockSpec(memory_space=pltpu.VMEM)
SMEM = pl.BlockSpec(memory_space=pltpu.SMEM)
F32 = jnp.float32


def params(mib=48):
    return pltpu.CompilerParams(vmem_limit_bytes=mib * 1024 * 1024)


def turned_shape(blocks=RB):
    return jax.ShapeDtypeStruct((PEERS, blocks, 8, 128), F32)


def gradients(st, top, bottom, left, right, rb, k):
    rows = pl.ds(rb * 8, 8)
    x = st[k, rows]
    before = st[k, jnp.maximum(rb * 8 - 1, 0)]
    before = jnp.where(rb == 0, jnp.zeros_like(before) if top is None else top[2 + k], before)
    after = st[k, jnp.minimum(rb * 8 + 8, 95)]
    after = jnp.where(rb == RB - 1, jnp.zeros_like(after) if bottom is None else bottom[3 + k], after)
    up = jnp.concatenate([x[1:], after[None]], axis=0)
    down = jnp.concatenate([before[None], x[:-1]], axis=0)
    col = lax.broadcasted_iota(jnp.int32, x.shape, 1)
    lo = 0.0 if left is None else left[k, rows][:, None, :]
    hi = 0.0 if right is None else right[k, rows][:, None, :]
    nxt = jnp.where(col == 15, hi, pltpu.roll(x, 15, 1))
    prv = jnp.where(col == 0, lo, pltpu.roll(x, 1, 1))
    return (
        (up - down) * 0.5,
        (nxt - prv) * 0.5,
        (pltpu.roll(x, 127, 2) - pltpu.roll(x, 1, 2)) * 0.5,
    )


def turn(x):
    return x.reshape(128, 128).T.reshape(PEERS, 8, 128)


def contract(v, g):
    return -0.5 * (v[0] * g[0] + v[1] * g[1] + v[2] * g[2])


CHUNKS = 4


def pre_kernel(v_hbm, st_hbm, out0, out1, sides, to_prv, to_nxt, v, st, sems):
    rows = 96 // CHUNKS
    copies = [pltpu.make_async_copy(st_hbm.at[k], st.at[k], sems.at[k]) for k in range(2)]
    for i in range(CHUNKS):
        part = pl.ds(i * rows, rows)
        copies.append(pltpu.make_async_copy(v_hbm.at[:, part], v.at[:, part], sems.at[2 + i]))
    for c in copies:
        c.start()
    copies[0].wait()
    copies[1].wait()
    for i in range(CHUNKS):
        copies[2 + i].wait()

        @pl.loop(i * RB // CHUNKS, (i + 1) * RB // CHUNKS)
        def _(rb):
            block = pl.ds(rb * 8, 8)
            vb = v[:, block]
            a = contract(vb, gradients(st, None, None, None, None, rb, 0))
            out0[:, rb] = turn(a)
            out1[:, rb] = turn(contract(vb, gradients(st, None, None, None, None, rb, 1)))
            sides[0, block] = 0.25 * vb[1, :, 0]
            sides[1, block] = -0.25 * vb[1, :, 15]

            @pl.when(rb == 0)
            def _():
                to_prv[0] = a[0]
                to_prv[2] = a[1]

            @pl.when(rb == RB - 1)
            def _():
                to_nxt[0] = a[7]

    to_prv[1] = v[0, 0]
    to_prv[3] = st[0, 0]
    to_prv[4] = st[1, 0]
    to_nxt[1] = v[0, 95]
    to_nxt[2] = st[0, 95]
    to_nxt[3] = st[1, 95]


def in_hbm(x):
    return pltpu.with_memory_space_constraint(x, pltpu.HBM)


def pre(velocity, states):
    hbm = pl.BlockSpec(memory_space=pltpu.HBM)
    return pl.pallas_call(
        pre_kernel,
        in_specs=[hbm, hbm],
        out_specs=[VMEM] * 5,
        out_shape=[
            turned_shape(RB + 1),
            turned_shape(),
            jax.ShapeDtypeStruct((2, 96, 128), F32),
            jax.ShapeDtypeStruct((5, 16, 128), F32),
            jax.ShapeDtypeStruct((4, 16, 128), F32),
        ],
        scratch_shapes=[
            pltpu.VMEM((3, 96, 16, 128), F32),
            pltpu.VMEM((2, 96, 16, 128), F32),
            pltpu.SemaphoreType.DMA((2 + CHUNKS,)),
        ],
        compiler_params=params(24),
        cost_estimate=COST,
        name="pre",
    )(in_hbm(velocity), in_hbm(states))


def rims_kernel(prv, nxt, sides, left, right, to_prv, to_nxt):
    col = lax.broadcasted_iota(jnp.int32, (16, 128), 0)

    def side(row):
        lo = sides[0, row : row + 1] * left[0, row : row + 1]
        hi = sides[1, row : row + 1] * right[0, row : row + 1]
        return jnp.where(col == 0, lo, 0.0) + jnp.where(col == 15, hi, 0.0)

    to_prv[0] = prv[0] + side(0)
    to_prv[1] = prv[1]
    to_prv[2] = prv[2] + side(1)
    to_prv[3] = prv[3]
    to_prv[4] = prv[4]
    to_nxt[0] = nxt[0] + side(95)
    to_nxt[1] = nxt[1]
    to_nxt[2] = nxt[2]
    to_nxt[3] = nxt[3]


def rims(prv, nxt, sides, left, right):
    return pl.pallas_call(
        rims_kernel,
        in_specs=[VMEM] * 5,
        out_specs=[VMEM, VMEM],
        out_shape=[jax.ShapeDtypeStruct((5, 16, 128), F32), jax.ShapeDtypeStruct((4, 16, 128), F32)],
        compiler_params=params(16),
        name="rims",
    )(prv, nxt, sides, left, right)


def columns_kernel(a0, a1, sides, left, right, out0, out1):
    col = lax.broadcasted_iota(jnp.int32, (8, 16, 128), 1)
    for k, (a, out) in enumerate(((a0, out0), (a1, out1))):
        for j in range(3):
            rows = pl.ds(8 * j, 8)
            lo = (sides[0, rows] * left[k, rows])[:, None, :]
            hi = (sides[1, rows] * right[k, rows])[:, None, :]
            out[:, j] = a[:, j] + turn(jnp.where(col == 0, lo, 0.0) + jnp.where(col == 15, hi, 0.0))


def columns(a0, a1, sides, left, right):
    block = pl.BlockSpec((PEERS, 3, 8, 128), lambda i: (0, i, 0, 0))
    side = pl.BlockSpec((2, 24, 128), lambda i: (0, i, 0))
    return pl.pallas_call(
        columns_kernel,
        grid=(RB // 3,),
        in_specs=[block, block, side, side, side],
        out_specs=[block, block],
        out_shape=[turned_shape(RB + 1), turned_shape()],
        input_output_aliases={0: 0, 1: 1},
        compiler_params=params(16),
        cost_estimate=COST,
        name="columns",
    )(a0, a1, sides, left, right)


def whole(shape):
    return pl.BlockSpec(shape, lambda i: (0,) * len(shape))


def natural3(f):
    return pl.BlockSpec((3, 8, 16, 128), lambda i: (0, f(i), 0, 0))


def turned(f):
    return pl.BlockSpec((PEERS, 1, 8, 128), lambda i: (0, f(i), 0, 0))


def same(i):
    return i


COST = pl.CostEstimate(flops=20_000_000, bytes_accessed=6_000_000, transcendentals=0)


def close_kernel(a0, a1, my_prv, my_nxt, from_nxt, from_prv, table, out0, out1):
    i = pl.program_id(0)
    row = lax.broadcasted_iota(jnp.int32, (8, 16, 128), 0)
    zero = jnp.zeros((8, 16, 128), F32)
    lane = lax.broadcasted_iota(jnp.int32, (PEERS, 8, 128), 2)

    @pl.when(i == 0)
    def _():
        for k, (a, out) in enumerate(((a0, out0), (a1, out1))):
            x = 0.25 * my_prv[1] * from_prv[2 + k]
            out[:, 0] = a[:, 0] + turn(jnp.where(row == 0, x[None], zero))

    @pl.when(i == 1)
    def _():
        for k, (a, out) in enumerate(((a0, out0), (a1, out1))):
            x = -0.25 * my_nxt[1] * from_nxt[3 + k]
            out[:, 0] = a[:, 0] + turn(jnp.where(row == 7, x[None], zero))

    @pl.when(i == 2)
    def _():
        before = from_prv[0] - 0.25 * from_prv[1] * my_prv[3]
        after = from_nxt[0] + 0.25 * from_nxt[1] * my_nxt[2]
        x = jnp.where(row == 7, before[None], zero)
        x = jnp.where(row == 0, after[None], x)
        x = jnp.where(row == 1, from_nxt[2][None], x)
        inner = (lane >= 32) & (lane < 112)
        out0[:, 0] = jnp.where(inner, table[...][None], turn(x))


def close(a0, a1, my_prv, my_nxt, from_nxt, from_prv, table):
    def block(i):
        return jnp.minimum(i * (RB - 1), RB)

    def kept(i):
        return jnp.minimum(i * (RB - 1), RB - 1)

    return pl.pallas_call(
        close_kernel,
        grid=(3,),
        in_specs=[
            turned(block),
            turned(kept),
            whole((5, 16, 128)),
            whole((4, 16, 128)),
            whole((5, 16, 128)),
            whole((4, 16, 128)),
            whole((1, 128)),
        ],
        out_specs=[turned(block), turned(kept)],
        out_shape=[turned_shape(RB + 1), turned_shape()],
        input_output_aliases={0: 0, 1: 1},
        compiler_params=params(16),
        name="close",
    )(a0, a1, my_prv, my_nxt, from_nxt, from_prv, table)


def force_block(adj1, adj0, st, edges, rb, out):
    b1 = (adj1.reshape(128, 128).T * -0.5).reshape(8, 16, 128)
    b0 = (adj0.reshape(128, 128).T * -0.5).reshape(8, 16, 128)
    g1 = gradients(st, *edges, rb, 1)
    g0 = gradients(st, *edges, rb, 0)
    for c in range(3):
        out[c] = b1 * g1[c] + b0 * g0[c]


def force_kernel(adj1, adj0, st, top, bottom, left, right, out):
    force_block(adj1[:, 0], adj0[:, 0], st, (top, bottom, left, right), pl.program_id(0) + 1, out)


def force_edge_kernel(adj1, adj0, st, top, bottom, left, right, from_nxt, from_prv, prior, out):
    i = pl.program_id(0)
    lane = lax.broadcasted_iota(jnp.int32, (PEERS, 8, 128), 2)
    x = jnp.where((i == 0) & (lane < 32), from_prv[...], 0.0)
    x = x + jnp.where((i == 1) & (lane >= 112), from_nxt[...], 0.0)
    force_block(adj1[:, 0], adj0[:, 0] + x, st, (top, bottom, left, right), i * (RB - 1), out)


def force(adj1, adj0, states, edges):
    fixed = [whole((2, 96, 16, 128)), whole((4, 16, 128)), whole((5, 16, 128)), whole((2, 96, 128)), whole((2, 96, 128))]
    shape = jax.ShapeDtypeStruct((3, 96, 16, 128), F32)
    rim = adj0[:, RB]
    from_nxt = to_prev(rim, "gx", lax.axis_size("gx"))
    from_prv = to_next(rim, "gx", lax.axis_size("gx"))
    args = (adj1, adj0, states, *edges)

    def inner(i):
        return i + 1

    def outer(i):
        return i * (RB - 1)

    main = pl.pallas_call(
        force_kernel,
        grid=(RB - 2,),
        in_specs=[turned(inner), turned(inner)] + fixed,
        out_specs=natural3(inner),
        out_shape=shape,
        compiler_params=params(24),
        cost_estimate=COST,
        name="force",
    )(*args)
    return pl.pallas_call(
        force_edge_kernel,
        grid=(2,),
        in_specs=[turned(outer), turned(outer)]
        + fixed
        + [whole((PEERS, 8, 128)), whole((PEERS, 8, 128)), pl.BlockSpec(memory_space=pl.ANY)],
        out_specs=natural3(outer),
        out_shape=shape,
        input_output_aliases={9: 0},
        compiler_params=params(24),
        name="force_edge",
    )(*args, from_nxt, from_prv, main)


def lanes():
    return lax.broadcasted_iota(jnp.int32, (8, 128), 1)


def split(x):
    hi = x.astype(BF16)
    return hi, (x - hi.astype(F32)).astype(BF16)


def load_taps(lhs, taps, e, x):
    col = lax.broadcasted_iota(jnp.int32, x.shape, 2) % 16
    after = jnp.concatenate([x[1:], x[:1]], axis=0)
    before = jnp.concatenate([x[-1:], x[:-1]], axis=0)
    xh, xl = split(x.reshape(128, 128))
    eh, el = split(jnp.where(col < 2, after, before).reshape(128, 128))
    rows = pl.ds(e * 128, 128)
    lhs[rows, 0:128] = xh
    lhs[rows, 128:256] = eh
    lhs[rows, 256:384] = xl
    lhs[rows, 384:512] = el
    taps[1, pl.ds(e * PEERS, PEERS)] = x


def shift_taps(lhs, shift, taps, blocks):
    m = shift[...]
    y = jnp.dot(lhs[0 : blocks * 128, 0:512], jnp.concatenate([m, m], axis=0), preferred_element_type=F32)
    for n, t in enumerate((0, 2, 3)):
        taps[t, 0 : blocks * PEERS] = y[:, n * 128 : n * 128 + 128].reshape(blocks * PEERS, 8, 128)


def shift_taps_adjoint(lhs, shift_t, acc, put):
    @pl.loop(0, RB + 2)
    def _(e):
        rows = pl.ds(e * 128, 128)
        for n, t in enumerate((0, 2, 3)):
            h, l = split(acc[t, pl.ds(e * PEERS, PEERS)].reshape(128, 128))
            lhs[rows, n * 128 : n * 128 + 128] = h
            lhs[rows, 384 + n * 128 : 512 + n * 128] = l

    m = shift_t[...]
    y = jnp.dot(lhs[...], jnp.concatenate([m, m], axis=0), preferred_element_type=F32)
    col = lax.broadcasted_iota(jnp.int32, (PEERS, 8, 128), 2) % 16
    for e in range(RB + 2):
        own = y[e * 128 : e * 128 + 128, :128].reshape(PEERS, 8, 128)
        rim = y[e * 128 : e * 128 + 128, 128:].reshape(PEERS, 8, 128)
        after = jnp.concatenate([rim[-1:], rim[:-1]], axis=0)
        before = jnp.concatenate([rim[1:], rim[:1]], axis=0)
        put(e, acc[1, e * PEERS : (e + 1) * PEERS] + own + jnp.where(col < 2, after, before))


def fill_weights(wv, values):
    for f in range(QF):
        for t in range(4):
            wv[f, t] = jnp.full((8, 128), float(values[f, t]), F32)


def brick_plan(tab, wv, b):
    base = tab[0, b]
    u = tab[1, b]
    v = tab[2, b]
    return base, [wv[u, t] for t in range(4)], [wv[v, t] for t in range(4)]


def brick_columns(taps, base, wc):
    c = []
    for i in range(4):
        acc = [wc[t] * taps[t, base + i * PEERS] for t in range(4)]
        c.append((acc[0] + acc[1]) + (acc[2] + acc[3]))
    return c


def brick_rows(wr, c):
    lane = lanes()
    outs = []
    for h in range(2):
        prv, cur, nxt = c[h], c[h + 1], c[h + 2]
        outs.append(
            (wr[0] * pltpu.roll(jnp.where(lane >= 112, prv, cur), 16, 1) + wr[1] * cur)
            + (
                wr[2] * pltpu.roll(jnp.where(lane < 16, nxt, cur), 112, 1)
                + wr[3] * pltpu.roll(jnp.where(lane < 32, nxt, cur), 96, 1)
            )
        )
    return outs


def brick_rows_adjoint(wr, v):
    lane = lanes()
    lo, own, hi = [], [], []
    for h in range(2):
        p0 = wr[0] * pltpu.roll(v[h], 112, 1)
        p2 = wr[2] * pltpu.roll(v[h], 16, 1)
        p3 = wr[3] * pltpu.roll(v[h], 32, 1)
        lo.append(jnp.where(lane >= 112, p0, 0.0))
        own.append(
            (wr[1] * v[h] + jnp.where(lane >= 112, 0.0, p0))
            + (jnp.where(lane < 16, 0.0, p2) + jnp.where(lane < 32, 0.0, p3))
        )
        hi.append(jnp.where(lane < 16, p2, 0.0) + jnp.where(lane < 32, p3, 0.0))
    return [lo[0], own[0] + lo[1], own[1] + hi[0], hi[1]]


def brick_add(acc, base, wc, c):
    for i in range(4):
        for t in range(4):
            acc[t, base + i * PEERS] = acc[t, base + i * PEERS] + wc[t] * c[i]


BUF = pltpu.VMEM((BRICKS, 4, 8, 128), F32)


def each_peer(first, second, bufs):
    for k in range(BRICKS):
        first(0, k, bufs[0])

    @pl.loop(0, PEERS // 2)
    def _(i):
        d = 2 * i
        for k in range(BRICKS):
            second(d, k, bufs[0])
            first(d + 1, k, bufs[1])
        for k in range(BRICKS):
            second(d + 1, k, bufs[1])
            first(jnp.minimum(d + 2, PEERS - 1), k, bufs[0])


def pull_kernel(tab, shift, x, out, taps, wv, lhs, *bufs):
    fill_weights(wv, WEIGHTS)
    load_taps(lhs, taps, 0, x[:, RB])

    @pl.loop(0, RB)
    def _(rb):
        load_taps(lhs, taps, rb + 1, x[:, rb])

    shift_taps(lhs, shift, taps, RB + 1)
    for t in range(4):
        taps[t, (RB + 1) * PEERS :] = taps[t, 0:PEERS]

    def first(d, k, buf):
        base, _, wc = brick_plan(tab, wv, d * BRICKS + k)
        c = brick_columns(taps, base, wc)
        for i in range(4):
            buf[k, i] = c[i]

    def second(d, k, buf):
        _, wr, _ = brick_plan(tab, wv, d * BRICKS + k)
        o = brick_rows(wr, [buf[k, i] for i in range(4)])
        for h in range(2):
            out[d, 2 * k + h] = o[h]

    each_peer(first, second, bufs)


TAPS = pltpu.VMEM((4, PEERS * (RB + 2), 8, 128), F32)
WV = pltpu.VMEM((QF, 4, 8, 128), F32)


LHS = pltpu.VMEM(((RB + 2) * 128, 768), BF16)


def pull(tab, shift, x):
    return pl.pallas_call(
        pull_kernel,
        in_specs=[SMEM, VMEM, VMEM],
        out_specs=VMEM,
        out_shape=turned_shape(),
        scratch_shapes=[TAPS, WV, LHS, BUF, BUF],
        compiler_params=params(24),
        name="pull",
    )(tab, shift, x)


def clear(acc):
    @pl.loop(0, RB + 2)
    def _(e):
        acc[:, pl.ds(e * PEERS, PEERS)] = jnp.zeros((4, PEERS, 8, 128), F32)


def push_kernel(tab, shift_t, v, st_hbm, out, st, acc, wv, lhs, buf_a, buf_b, sem):
    copy = pltpu.make_async_copy(st_hbm, st, sem)
    copy.start()
    fill_weights(wv, WEIGHTS)
    clear(acc)

    def first(d, k, buf):
        _, wr, _ = brick_plan(tab, wv, d * BRICKS + k)
        c = brick_rows_adjoint(wr, [v[d, 2 * k], v[d, 2 * k + 1]])
        for i in range(4):
            buf[k, i] = c[i]

    def second(d, k, buf):
        base, _, wc = brick_plan(tab, wv, d * BRICKS + k)
        brick_add(acc, base, wc, [buf[k, i] for i in range(4)])

    each_peer(first, second, (buf_a, buf_b))

    def put(e, block):
        if e == 0:
            out[:, RB] = block
        elif e == RB + 1:
            out[:, RB] = out[:, RB] + block
        else:
            out[:, e - 1] = block

    shift_taps_adjoint(lhs, shift_t, acc, put)
    copy.wait()


def push(tab, shift_t, v, states):
    return pl.pallas_call(
        push_kernel,
        in_specs=[SMEM, VMEM, VMEM, pl.BlockSpec(memory_space=pltpu.HBM)],
        out_specs=[VMEM, VMEM],
        out_shape=[turned_shape(RB + 1), jax.ShapeDtypeStruct(states.shape, F32)],
        scratch_shapes=[TAPS, WV, LHS, BUF, BUF, pltpu.SemaphoreType.DMA],
        compiler_params=params(24),
        name="push",
    )(tab, shift_t, v, in_hbm(states))


def normal_kernel(tab, shift, shift_t, x, prv, nxt, out, lo, hi, taps, acc, wv, kv, lhs, *bufs):
    fill_weights(wv, WEIGHTS)
    fill_weights(kv, PAIRS)
    clear(acc)
    sub3 = lax.broadcasted_iota(jnp.int32, (PEERS, 8, 128), 1) < 3
    last = 8 * RB + 6 * (RB - 1) - 2

    def block(e):
        if e == 0:
            return prv[:, 0:8], pltpu.roll(prv[:, 8:16], 6, 1)
        if e == RB + 1:
            return nxt[:, 0:8], nxt[:, 8:16]
        if e == RB:
            return x[:, 8 * RB - 8 : 8 * RB], pltpu.roll(x[:, last : last + 8], 6, 1)
        return x[:, 8 * e - 8 : 8 * e], x[:, 8 * RB + 6 * (e - 1) : 8 * RB + 6 * (e - 1) + 8]

    for q in range(2):
        for e in range(RB + 2):
            own, rim = block(e)
            own = pltpu.roll(own, 3, 1)
            tile = jnp.where(sub3, rim, own) if q == 0 else jnp.where(sub3, own, rim)
            load_taps(lhs, taps.at[q], e, tile)
        shift_taps(lhs, shift, taps.at[q], RB + 2)

    def first(d, k, buf):
        sub = lax.broadcasted_iota(jnp.int32, (8, 128), 0)
        base, _, wc = brick_plan(tab, wv, d * BRICKS + k)
        c0 = brick_columns(taps.at[0], base, wc)
        c1 = brick_columns(taps.at[1], base, wc)
        f = tab[3, d * BRICKS + k]
        kw = [kv[f, t] for t in range(4)]
        for i in range(4):
            at = [c0[i]] + [pltpu.roll(jnp.where(sub >= a, c0[i], c1[i]), 8 - a, 0) for a in range(1, 7)]
            near = kw[0] * at[3] + kw[1] * (at[2] + at[4])
            buf[k, i] = near + (kw[2] * (at[1] + at[5]) + kw[3] * (at[0] + at[6]))

    def second(d, k, buf):
        base, wr, wc = brick_plan(tab, wv, d * BRICKS + k)
        c = brick_rows_adjoint(wr, brick_rows(wr, [buf[k, i] for i in range(4)]))
        brick_add(acc, base, wc, c)

    each_peer(first, second, bufs)

    def put(e, block):
        if e == 0:
            lo[...] = block
        elif e == RB + 1:
            hi[...] = block
        else:
            out[:, e - 1] = block

    shift_taps_adjoint(lhs, shift_t, acc, put)


EDGE = jax.ShapeDtypeStruct((PEERS, 8, 128), F32)


def normal(tab, shift, shift_t, x, prv, nxt):
    return pl.pallas_call(
        normal_kernel,
        in_specs=[SMEM, VMEM, VMEM, VMEM, VMEM, VMEM],
        out_specs=[VMEM, VMEM, VMEM],
        out_shape=[turned_shape(), EDGE, EDGE],
        scratch_shapes=[
            pltpu.VMEM((2, 4, PEERS * (RB + 2), 8, 128), F32),
            TAPS,
            WV,
            WV,
            LHS,
            BUF,
            BUF,
        ],
        compiler_params=params(24),
        name="normal",
    )(tab, shift, shift_t, x, prv, nxt)


def depth_matrix(q, transpose):
    n = q // QF
    f = (q % QF).astype(F32) * (1.0 / QF)
    weights = (
        f * (f - 1.0) * (f - 2.0) * (-1.0 / 6.0),
        (f + 1.0) * (f - 1.0) * (f - 2.0) * 0.5,
        (f + 1.0) * f * (f - 2.0) * -0.5,
        (f + 1.0) * f * (f - 1.0) * (1.0 / 6.0),
    )
    i = lax.broadcasted_iota(jnp.int32, (128, 128), 0)
    j = lax.broadcasted_iota(jnp.int32, (128, 128), 1)
    off = (i - j if transpose else j - i) + (257 - n)
    off = jnp.bitwise_and(off, 127)
    w = jnp.zeros((128, 128), F32)
    for m in range(4):
        w = jnp.where(off == m, weights[m], w)
    return w


def depth_product(q, transpose, r, k):
    wh, wl = split(depth_matrix(q, transpose))
    xh, xl = split(jnp.concatenate([r[:, 2 * k + h].reshape(128, 128) for h in range(2)], axis=1))
    y = jnp.dot(
        jnp.concatenate([wh, wl, wh], axis=1), jnp.concatenate([xh, xh, xl], axis=0), preferred_element_type=F32
    )
    return y[:, :128], y[:, 128:]


PACKED = 8 * RB + 6 * RB


def depth_kernel(code, r, a, out):
    sub = lax.broadcasted_iota(jnp.int32, (PEERS, 8, 128), 1)
    for k in range(BRICKS):
        ys = depth_product(code[k], False, r, k)
        for h in range(2):
            rb = 2 * k + h
            tiles = ys[h].reshape(PEERS, 8, 128) + a[:, rb]
            out[:, 8 * rb : 8 * rb + 8] = tiles
            moved = pltpu.roll(tiles, 3, 1)
            before = jnp.concatenate([moved[-1:], moved[:-1]], axis=0)
            after = jnp.concatenate([moved[1:], moved[:1]], axis=0)
            rim = jnp.where(sub < 3, before, after)
            out[:, 8 * RB + 6 * rb : 8 * RB + 6 * rb + 6] = rim[:, :6]


def depth(code, r, a):
    return pl.pallas_call(
        depth_kernel,
        in_specs=[SMEM, VMEM, VMEM],
        out_specs=VMEM,
        out_shape=jax.ShapeDtypeStruct((PEERS, PACKED, 128), F32),
        compiler_params=params(24),
        name="depth",
    )(code, r, a)


def depth_adjoint_kernel(code, r, out):
    for k in range(BRICKS):
        ys = depth_product(code[k], True, r, k)
        for h in range(2):
            out[:, 2 * k + h] = ys[h].reshape(PEERS, 8, 128)


def depth_adjoint(code, r):
    return pl.pallas_call(
        depth_adjoint_kernel,
        in_specs=[SMEM, VMEM],
        out_specs=VMEM,
        out_shape=turned_shape(),
        compiler_params=params(24),
        name="depth_adjoint",
    )(code, r)


def to_next(x, axis, count):
    return lax.ppermute(x, axis, [(i, (i + 1) % count) for i in range(count)])


def to_prev(x, axis, count):
    return lax.ppermute(x, axis, [((i + 1) % count, i) for i in range(count)])


def swap(x):
    return lax.all_to_all(x, "gy", split_axis=0, concat_axis=0, tiled=True)


def brick_table(raw):
    t = raw.astype(jnp.int32)
    slot = t[:, 32:38]
    sends = t[:, :32].reshape(PEERS, PEERS, 2).transpose(1, 0, 2).reshape(PEERS, 1, 32)
    hit = slot[:, :, None] == jnp.arange(32)[None, None, :]
    local = jnp.sum(jnp.where(hit, sends, 0), axis=2)
    rows = [2 * PEERS * local + slot // 2, t[:, 38:44], t[:, 44:50], t[:, 50:56] % QF]
    return jnp.stack(rows).reshape(4, PEERS * BRICKS)


def body(velocity, states, pull_plan, send_plan, codes):
    gx = lax.axis_size("gx")
    gy = lax.axis_size("gy")
    left = to_next(states[:, :, -1], "gy", gy)
    right = to_prev(states[:, :, 0], "gy", gy)
    a0, a1, sides, my_prv, my_nxt = pre(velocity, states)
    shift = jnp.asarray(SHIFT, BF16)
    shift_t = jnp.asarray(SHIFT.T, BF16)
    code = codes[2].reshape(BRICKS)
    mine = [send_plan.reshape(32), pull_plan.reshape(BRICKS), codes.reshape(3 * BRICKS)]
    table = jnp.concatenate([jnp.zeros((32,), jnp.int32)] + mine + [jnp.zeros((40,), jnp.int32)])
    table = table.astype(F32).reshape(1, 128)

    my_prv, my_nxt = rims(my_prv, my_nxt, sides, left, right)
    from_nxt = to_prev(my_prv, "gx", gx)
    from_prv = to_next(my_nxt, "gx", gx)
    a0, a1 = columns(a0, a1, sides, left, right)
    a0, a1 = close(a0, a1, my_prv, my_nxt, from_nxt, from_prv, table)
    a0, code = lax.optimization_barrier((a0, code))
    x = swap(a0)
    tab = brick_table(x[:, RB, 0, 32:88])
    r = swap(pull(tab, shift, x))
    u = swap(depth(code, r, a1))
    low = jnp.concatenate([u[:, 8 * RB - 8 : 8 * RB], u[:, PACKED - 8 :]], axis=1)
    high = jnp.concatenate([u[:, :8], u[:, 8 * RB : 8 * RB + 8]], axis=1)
    y, lo, hi = normal(tab, shift, shift_t, u, to_next(low, "gx", gx), to_prev(high, "gx", gx))
    y = y.at[:, RB - 1].add(to_prev(lo, "gx", gx)).at[:, 0].add(to_next(hi, "gx", gx))
    adj1 = swap(y)
    v = swap(depth_adjoint(code, adj1))
    y, states = push(tab, shift_t, v, states)
    adj0 = swap(y)
    return force(adj1, adj0, states, (from_prv, from_nxt, left, right))


def solution(mesh):
    return jax.shard_map(
        body,
        mesh=mesh,
        in_specs=(
            P(None, "gx", "gy", None),
            P(None, "gx", "gy", None),
            P("gx", "gy"),
            P("gx", "gy", None, None),
            P(None, "gx", "gy"),
        ),
        out_specs=P(None, "gx", "gy", None),
        check_vma=False,
    )
```

```python
import functools

import jax
import jax.numpy as jnp
import numpy as np
from jax import lax
from jax.experimental import pallas as pl
from jax.experimental.pallas import tpu as pltpu
from jax.sharding import PartitionSpec as P

QF = 8
PEERS = 16
RB = 12
BRICKS = 6


def weights_of(f):
    return np.array(
        [
            -f * (f - 1.0) * (f - 2.0) / 6.0,
            (f + 1.0) * (f - 1.0) * (f - 2.0) / 2.0,
            -(f + 1.0) * f * (f - 2.0) / 2.0,
            (f + 1.0) * f * (f - 1.0) / 6.0,
        ]
    )


WEIGHTS = np.stack([weights_of(k / QF) for k in range(QF)])
PAIRS = np.stack([[np.dot(w[: 4 - d], w[d:]) for d in range(4)] for w in WEIGHTS])


def shift_matrix():
    m = np.zeros((2, 8, 16, 3, 8, 16), np.float32)
    for r in range(8):
        for j in range(16):
            for n, d in enumerate((-1, 1, 2)):
                inside = 0 <= j + d < 16
                m[0 if inside else 1, r, (j + d) % 16, n, r, j] = 1.0
    return m.reshape(256, 384)


SHIFT = shift_matrix()
BF16 = jnp.bfloat16

VMEM = pl.BlockSpec(memory_space=pltpu.VMEM)
SMEM = pl.BlockSpec(memory_space=pltpu.SMEM)
F32 = jnp.float32


def params(mib=48):
    return pltpu.CompilerParams(vmem_limit_bytes=mib * 1024 * 1024)


def turned_shape(blocks=RB):
    return jax.ShapeDtypeStruct((PEERS, blocks, 8, 128), F32)


def gradients(st, top, bottom, left, right, rb, k):
    rows = pl.ds(rb * 8, 8)
    x = st[k, rows]
    fixed = isinstance(rb, int)
    before = st[k, max(rb * 8 - 1, 0) if fixed else jnp.maximum(rb * 8 - 1, 0)]
    before = jnp.where(rb == 0, jnp.zeros_like(before) if top is None else top[2 + k], before)
    after = st[k, min(rb * 8 + 8, 95) if fixed else jnp.minimum(rb * 8 + 8, 95)]
    after = jnp.where(rb == RB - 1, jnp.zeros_like(after) if bottom is None else bottom[3 + k], after)
    up = jnp.concatenate([x[1:], after[None]], axis=0)
    down = jnp.concatenate([before[None], x[:-1]], axis=0)
    col = lax.broadcasted_iota(jnp.int32, x.shape, 1)
    lo = 0.0 if left is None else left[k, rows][:, None, :]
    hi = 0.0 if right is None else right[k, rows][:, None, :]
    nxt = jnp.where(col == 15, hi, pltpu.roll(x, 15, 1))
    prv = jnp.where(col == 0, lo, pltpu.roll(x, 1, 1))
    return (
        (up - down) * 0.5,
        (nxt - prv) * 0.5,
        (pltpu.roll(x, 127, 2) - pltpu.roll(x, 1, 2)) * 0.5,
    )


def turn(x):
    return x.reshape(128, 128).T.reshape(PEERS, 8, 128)


def contract(v, g):
    return -0.5 * (v[0] * g[0] + v[1] * g[1] + v[2] * g[2])


CHUNKS = 4


def pre_kernel(v_hbm, st_hbm, out0, out1, sides, to_prv, to_nxt, v, st, sems):
    rows = 96 // CHUNKS
    copies = [pltpu.make_async_copy(st_hbm.at[k], st.at[k], sems.at[k]) for k in range(2)]
    for i in range(CHUNKS):
        part = pl.ds(i * rows, rows)
        copies.append(pltpu.make_async_copy(v_hbm.at[:, part], v.at[:, part], sems.at[2 + i]))
    for c in copies:
        c.start()
    copies[0].wait()
    copies[1].wait()
    for i in range(CHUNKS):
        copies[2 + i].wait()

        @pl.loop(i * RB // CHUNKS, (i + 1) * RB // CHUNKS)
        def _(rb):
            block = pl.ds(rb * 8, 8)
            vb = v[:, block]
            a = contract(vb, gradients(st, None, None, None, None, rb, 0))
            out0[:, rb] = turn(a)
            out1[:, rb] = turn(contract(vb, gradients(st, None, None, None, None, rb, 1)))
            sides[0, block] = 0.25 * vb[1, :, 0]
            sides[1, block] = -0.25 * vb[1, :, 15]

            @pl.when(rb == 0)
            def _():
                to_prv[0] = a[0]
                to_prv[2] = a[1]

            @pl.when(rb == RB - 1)
            def _():
                to_nxt[0] = a[7]

    to_prv[1] = v[0, 0]
    to_prv[3] = st[0, 0]
    to_prv[4] = st[1, 0]
    to_nxt[1] = v[0, 95]
    to_nxt[2] = st[0, 95]
    to_nxt[3] = st[1, 95]


def in_hbm(x):
    return pltpu.with_memory_space_constraint(x, pltpu.HBM)


def pre(velocity, states):
    hbm = pl.BlockSpec(memory_space=pltpu.HBM)
    return pl.pallas_call(
        pre_kernel,
        in_specs=[hbm, hbm],
        out_specs=[VMEM] * 5,
        out_shape=[
            turned_shape(RB + 1),
            turned_shape(),
            jax.ShapeDtypeStruct((2, 96, 128), F32),
            jax.ShapeDtypeStruct((5, 16, 128), F32),
            jax.ShapeDtypeStruct((4, 16, 128), F32),
        ],
        scratch_shapes=[
            pltpu.VMEM((3, 96, 16, 128), F32),
            pltpu.VMEM((2, 96, 16, 128), F32),
            pltpu.SemaphoreType.DMA((2 + CHUNKS,)),
        ],
        compiler_params=params(24),
        cost_estimate=COST,
        name="pre",
    )(in_hbm(velocity), in_hbm(states))


def rims_kernel(prv, nxt, sides, left, right, to_prv, to_nxt):
    col = lax.broadcasted_iota(jnp.int32, (16, 128), 0)

    def side(row):
        lo = sides[0, row : row + 1] * left[0, row : row + 1]
        hi = sides[1, row : row + 1] * right[0, row : row + 1]
        return jnp.where(col == 0, lo, 0.0) + jnp.where(col == 15, hi, 0.0)

    to_prv[0] = prv[0] + side(0)
    to_prv[1] = prv[1]
    to_prv[2] = prv[2] + side(1)
    to_prv[3] = prv[3]
    to_prv[4] = prv[4]
    to_nxt[0] = nxt[0] + side(95)
    to_nxt[1] = nxt[1]
    to_nxt[2] = nxt[2]
    to_nxt[3] = nxt[3]


def rims(prv, nxt, sides, left, right):
    return pl.pallas_call(
        rims_kernel,
        in_specs=[VMEM] * 5,
        out_specs=[VMEM, VMEM],
        out_shape=[jax.ShapeDtypeStruct((5, 16, 128), F32), jax.ShapeDtypeStruct((4, 16, 128), F32)],
        compiler_params=params(16),
        name="rims",
    )(prv, nxt, sides, left, right)


def columns_kernel(a0, a1, sides, left, right, out0, out1):
    col = lax.broadcasted_iota(jnp.int32, (8, 16, 128), 1)
    for k, (a, out) in enumerate(((a0, out0), (a1, out1))):
        for j in range(3):
            rows = pl.ds(8 * j, 8)
            lo = (sides[0, rows] * left[k, rows])[:, None, :]
            hi = (sides[1, rows] * right[k, rows])[:, None, :]
            out[:, j] = a[:, j] + turn(jnp.where(col == 0, lo, 0.0) + jnp.where(col == 15, hi, 0.0))


def columns(a0, a1, sides, left, right):
    block = pl.BlockSpec((PEERS, 3, 8, 128), lambda i: (0, i, 0, 0))
    side = pl.BlockSpec((2, 24, 128), lambda i: (0, i, 0))
    return pl.pallas_call(
        columns_kernel,
        grid=(RB // 3,),
        in_specs=[block, block, side, side, side],
        out_specs=[block, block],
        out_shape=[turned_shape(RB + 1), turned_shape()],
        input_output_aliases={0: 0, 1: 1},
        compiler_params=params(16),
        cost_estimate=COST,
        name="columns",
    )(a0, a1, sides, left, right)


def whole(shape):
    return pl.BlockSpec(shape, lambda i: (0,) * len(shape))


def natural3(f):
    return pl.BlockSpec((3, 8, 16, 128), lambda i: (0, f(i), 0, 0))


def turned(f):
    return pl.BlockSpec((PEERS, 1, 8, 128), lambda i: (0, f(i), 0, 0))


def same(i):
    return i


COST = pl.CostEstimate(flops=20_000_000, bytes_accessed=6_000_000, transcendentals=0)


def close_kernel(a0, a1, my_prv, my_nxt, from_nxt, from_prv, table, out0, out1):
    i = pl.program_id(0)
    row = lax.broadcasted_iota(jnp.int32, (8, 16, 128), 0)
    zero = jnp.zeros((8, 16, 128), F32)
    lane = lax.broadcasted_iota(jnp.int32, (PEERS, 8, 128), 2)

    @pl.when(i == 0)
    def _():
        for k, (a, out) in enumerate(((a0, out0), (a1, out1))):
            x = 0.25 * my_prv[1] * from_prv[2 + k]
            out[:, 0] = a[:, 0] + turn(jnp.where(row == 0, x[None], zero))

    @pl.when(i == 1)
    def _():
        for k, (a, out) in enumerate(((a0, out0), (a1, out1))):
            x = -0.25 * my_nxt[1] * from_nxt[3 + k]
            out[:, 0] = a[:, 0] + turn(jnp.where(row == 7, x[None], zero))

    @pl.when(i == 2)
    def _():
        before = from_prv[0] - 0.25 * from_prv[1] * my_prv[3]
        after = from_nxt[0] + 0.25 * from_nxt[1] * my_nxt[2]
        x = jnp.where(row == 7, before[None], zero)
        x = jnp.where(row == 0, after[None], x)
        x = jnp.where(row == 1, from_nxt[2][None], x)
        inner = (lane >= 32) & (lane < 112)
        out0[:, 0] = jnp.where(inner, table[...][None], turn(x))


def close(a0, a1, my_prv, my_nxt, from_nxt, from_prv, table):
    def block(i):
        return jnp.minimum(i * (RB - 1), RB)

    def kept(i):
        return jnp.minimum(i * (RB - 1), RB - 1)

    return pl.pallas_call(
        close_kernel,
        grid=(3,),
        in_specs=[
            turned(block),
            turned(kept),
            whole((5, 16, 128)),
            whole((4, 16, 128)),
            whole((5, 16, 128)),
            whole((4, 16, 128)),
            whole((1, 128)),
        ],
        out_specs=[turned(block), turned(kept)],
        out_shape=[turned_shape(RB + 1), turned_shape()],
        input_output_aliases={0: 0, 1: 1},
        compiler_params=params(16),
        name="close",
    )(a0, a1, my_prv, my_nxt, from_nxt, from_prv, table)


def force_block(adj1, adj0, st, edges, rb, out):
    b1 = (adj1.reshape(128, 128).T * -0.5).reshape(8, 16, 128)
    b0 = (adj0.reshape(128, 128).T * -0.5).reshape(8, 16, 128)
    g1 = gradients(st, *edges, rb, 1)
    g0 = gradients(st, *edges, rb, 0)
    for c in range(3):
        out[c] = b1 * g1[c] + b0 * g0[c]


def force_kernel(adj1, adj0, st, top, bottom, left, right, out_hbm, buf, sems):
    copies = []
    for n in range((RB - 2) // 2):
        for rb in (2 * n + 1, 2 * n + 2):
            rows = buf.at[:, pl.ds(8 * rb, 8)]
            force_block(adj1[:, rb], adj0[:, rb], st, (top, bottom, left, right), rb, rows)
        part = pl.ds(16 * n + 8, 16)
        copies.append(pltpu.make_async_copy(buf.at[:, part], out_hbm.at[:, part], sems.at[n]))
        copies[-1].start()
    for c in copies:
        c.wait()


def force_edge_kernel(adj1, adj0, st, top, bottom, left, right, from_nxt, from_prv, prior, out):
    i = pl.program_id(0)
    lane = lax.broadcasted_iota(jnp.int32, (PEERS, 8, 128), 2)
    x = jnp.where((i == 0) & (lane < 32), from_prv[...], 0.0)
    x = x + jnp.where((i == 1) & (lane >= 112), from_nxt[...], 0.0)
    force_block(adj1[:, 0], adj0[:, 0] + x, st, (top, bottom, left, right), i * (RB - 1), out)


def force(adj1, adj0, states, edges):
    fixed = [whole((2, 96, 16, 128)), whole((4, 16, 128)), whole((5, 16, 128)), whole((2, 96, 128)), whole((2, 96, 128))]
    shape = jax.ShapeDtypeStruct((3, 96, 16, 128), F32)
    rim = adj0[:, RB]
    from_nxt = to_prev(rim, "gx", lax.axis_size("gx"))
    from_prv = to_next(rim, "gx", lax.axis_size("gx"))
    args = (adj1, adj0, states, *edges)

    def outer(i):
        return i * (RB - 1)

    main = pl.pallas_call(
        force_kernel,
        in_specs=[VMEM] * 7,
        out_specs=pl.BlockSpec(memory_space=pltpu.HBM),
        out_shape=shape,
        scratch_shapes=[pltpu.VMEM((3, 96, 16, 128), F32), pltpu.SemaphoreType.DMA(((RB - 2) // 2,))],
        compiler_params=params(24),
        cost_estimate=COST,
        name="force",
    )(*args)
    return pl.pallas_call(
        force_edge_kernel,
        grid=(2,),
        in_specs=[turned(outer), turned(outer)]
        + fixed
        + [whole((PEERS, 8, 128)), whole((PEERS, 8, 128)), pl.BlockSpec(memory_space=pl.ANY)],
        out_specs=natural3(outer),
        out_shape=shape,
        input_output_aliases={9: 0},
        compiler_params=params(24),
        name="force_edge",
    )(*args, from_nxt, from_prv, main)


def lanes():
    return lax.broadcasted_iota(jnp.int32, (8, 128), 1)


def split(x):
    hi = x.astype(BF16)
    return hi, (x - hi.astype(F32)).astype(BF16)


def load_taps(lhs, taps, e, x):
    col = lax.broadcasted_iota(jnp.int32, x.shape, 2) % 16
    after = jnp.concatenate([x[1:], x[:1]], axis=0)
    before = jnp.concatenate([x[-1:], x[:-1]], axis=0)
    xh, xl = split(x.reshape(128, 128))
    eh, el = split(jnp.where(col < 2, after, before).reshape(128, 128))
    rows = pl.ds(e * 128, 128)
    lhs[rows, 0:128] = xh
    lhs[rows, 128:256] = eh
    lhs[rows, 256:384] = xl
    lhs[rows, 384:512] = el
    taps[1, pl.ds(e * PEERS, PEERS)] = x


def shift_taps(lhs, shift, taps, blocks):
    m = shift[...]
    y = jnp.dot(lhs[0 : blocks * 128, 0:512], jnp.concatenate([m, m], axis=0), preferred_element_type=F32)
    for n, t in enumerate((0, 2, 3)):
        taps[t, 0 : blocks * PEERS] = y[:, n * 128 : n * 128 + 128].reshape(blocks * PEERS, 8, 128)


def shift_taps_adjoint(lhs, shift_t, acc, put):
    @pl.loop(0, RB + 2)
    def _(e):
        rows = pl.ds(e * 128, 128)
        for n, t in enumerate((0, 2, 3)):
            h, l = split(acc[t, pl.ds(e * PEERS, PEERS)].reshape(128, 128))
            lhs[rows, n * 128 : n * 128 + 128] = h
            lhs[rows, 384 + n * 128 : 512 + n * 128] = l

    m = shift_t[...]
    y = jnp.dot(lhs[...], jnp.concatenate([m, m], axis=0), preferred_element_type=F32)
    col = lax.broadcasted_iota(jnp.int32, (PEERS, 8, 128), 2) % 16
    for e in range(RB + 2):
        own = y[e * 128 : e * 128 + 128, :128].reshape(PEERS, 8, 128)
        rim = y[e * 128 : e * 128 + 128, 128:].reshape(PEERS, 8, 128)
        after = jnp.concatenate([rim[-1:], rim[:-1]], axis=0)
        before = jnp.concatenate([rim[1:], rim[:1]], axis=0)
        put(e, acc[1, e * PEERS : (e + 1) * PEERS] + own + jnp.where(col < 2, after, before))


def fill_weights(wv, values):
    for f in range(QF):
        for t in range(4):
            wv[f, t] = jnp.full((8, 128), float(values[f, t]), F32)


def brick_plan(tab, wv, b):
    base = tab[0, b]
    u = tab[1, b]
    v = tab[2, b]
    return base, [wv[u, t] for t in range(4)], [wv[v, t] for t in range(4)]


def brick_columns(taps, base, wc):
    c = []
    for i in range(4):
        acc = [wc[t] * taps[t, base + i * PEERS] for t in range(4)]
        c.append((acc[0] + acc[1]) + (acc[2] + acc[3]))
    return c


def brick_rows(wr, c):
    lane = lanes()
    outs = []
    for h in range(2):
        prv, cur, nxt = c[h], c[h + 1], c[h + 2]
        outs.append(
            (wr[0] * pltpu.roll(jnp.where(lane >= 112, prv, cur), 16, 1) + wr[1] * cur)
            + (
                wr[2] * pltpu.roll(jnp.where(lane < 16, nxt, cur), 112, 1)
                + wr[3] * pltpu.roll(jnp.where(lane < 32, nxt, cur), 96, 1)
            )
        )
    return outs


def brick_rows_adjoint(wr, v):
    lane = lanes()
    lo, own, hi = [], [], []
    for h in range(2):
        p0 = wr[0] * pltpu.roll(v[h], 112, 1)
        p2 = wr[2] * pltpu.roll(v[h], 16, 1)
        p3 = wr[3] * pltpu.roll(v[h], 32, 1)
        lo.append(jnp.where(lane >= 112, p0, 0.0))
        own.append(
            (wr[1] * v[h] + jnp.where(lane >= 112, 0.0, p0))
            + (jnp.where(lane < 16, 0.0, p2) + jnp.where(lane < 32, 0.0, p3))
        )
        hi.append(jnp.where(lane < 16, p2, 0.0) + jnp.where(lane < 32, p3, 0.0))
    return [lo[0], own[0] + lo[1], own[1] + hi[0], hi[1]]


def brick_add(acc, base, wc, c):
    for i in range(4):
        for t in range(4):
            acc[t, base + i * PEERS] = acc[t, base + i * PEERS] + wc[t] * c[i]


BUF = pltpu.VMEM((BRICKS, 4, 8, 128), F32)


def each_peer(first, second, bufs):
    for k in range(BRICKS):
        first(0, k, bufs[0])

    @pl.loop(0, PEERS // 2)
    def _(i):
        d = 2 * i
        for k in range(BRICKS):
            second(d, k, bufs[0])
            first(d + 1, k, bufs[1])
        for k in range(BRICKS):
            second(d + 1, k, bufs[1])
            first(jnp.minimum(d + 2, PEERS - 1), k, bufs[0])


def pull_kernel(tab, shift, x, out, taps, wv, lhs, *bufs):
    fill_weights(wv, WEIGHTS)
    load_taps(lhs, taps, 0, x[:, RB])

    @pl.loop(0, RB)
    def _(rb):
        load_taps(lhs, taps, rb + 1, x[:, rb])

    shift_taps(lhs, shift, taps, RB + 1)
    for t in range(4):
        taps[t, (RB + 1) * PEERS :] = taps[t, 0:PEERS]

    def first(d, k, buf):
        base, _, wc = brick_plan(tab, wv, d * BRICKS + k)
        c = brick_columns(taps, base, wc)
        for i in range(4):
            buf[k, i] = c[i]

    def second(d, k, buf):
        _, wr, _ = brick_plan(tab, wv, d * BRICKS + k)
        o = brick_rows(wr, [buf[k, i] for i in range(4)])
        for h in range(2):
            out[d, 2 * k + h] = o[h]

    each_peer(first, second, bufs)


TAPS = pltpu.VMEM((4, PEERS * (RB + 2), 8, 128), F32)
WV = pltpu.VMEM((QF, 4, 8, 128), F32)


LHS = pltpu.VMEM(((RB + 2) * 128, 768), BF16)


def pull(tab, shift, x):
    return pl.pallas_call(
        pull_kernel,
        in_specs=[SMEM, VMEM, VMEM],
        out_specs=VMEM,
        out_shape=turned_shape(),
        scratch_shapes=[TAPS, WV, LHS, BUF, BUF],
        compiler_params=params(24),
        name="pull",
    )(tab, shift, x)


def clear(acc):
    @pl.loop(0, RB + 2)
    def _(e):
        acc[:, pl.ds(e * PEERS, PEERS)] = jnp.zeros((4, PEERS, 8, 128), F32)


def push_kernel(tab, shift_t, v, st_hbm, out, st, acc, wv, lhs, buf_a, buf_b, sem):
    copy = pltpu.make_async_copy(st_hbm, st, sem)
    copy.start()
    fill_weights(wv, WEIGHTS)
    clear(acc)

    def first(d, k, buf):
        _, wr, _ = brick_plan(tab, wv, d * BRICKS + k)
        c = brick_rows_adjoint(wr, [v[d, 2 * k], v[d, 2 * k + 1]])
        for i in range(4):
            buf[k, i] = c[i]

    def second(d, k, buf):
        base, _, wc = brick_plan(tab, wv, d * BRICKS + k)
        brick_add(acc, base, wc, [buf[k, i] for i in range(4)])

    each_peer(first, second, (buf_a, buf_b))

    def put(e, block):
        if e == 0:
            out[:, RB] = block
        elif e == RB + 1:
            out[:, RB] = out[:, RB] + block
        else:
            out[:, e - 1] = block

    shift_taps_adjoint(lhs, shift_t, acc, put)
    copy.wait()


def push(tab, shift_t, v, states):
    return pl.pallas_call(
        push_kernel,
        in_specs=[SMEM, VMEM, VMEM, pl.BlockSpec(memory_space=pltpu.HBM)],
        out_specs=[VMEM, VMEM],
        out_shape=[turned_shape(RB + 1), jax.ShapeDtypeStruct(states.shape, F32)],
        scratch_shapes=[TAPS, WV, LHS, BUF, BUF, pltpu.SemaphoreType.DMA],
        compiler_params=params(24),
        name="push",
    )(tab, shift_t, v, in_hbm(states))


def normal_kernel(tab, shift, shift_t, x, prv, nxt, out, lo, hi, taps, acc, wv, kv, lhs, *bufs):
    fill_weights(wv, WEIGHTS)
    fill_weights(kv, PAIRS)
    clear(acc)
    sub3 = lax.broadcasted_iota(jnp.int32, (PEERS, 8, 128), 1) < 3
    last = 8 * RB + 6 * (RB - 1) - 2

    def block(e):
        if e == 0:
            return prv[:, 0:8], pltpu.roll(prv[:, 8:16], 6, 1)
        if e == RB + 1:
            return nxt[:, 0:8], nxt[:, 8:16]
        if e == RB:
            return x[:, 8 * RB - 8 : 8 * RB], pltpu.roll(x[:, last : last + 8], 6, 1)
        return x[:, 8 * e - 8 : 8 * e], x[:, 8 * RB + 6 * (e - 1) : 8 * RB + 6 * (e - 1) + 8]

    for q in range(2):
        for e in range(RB + 2):
            own, rim = block(e)
            own = pltpu.roll(own, 3, 1)
            tile = jnp.where(sub3, rim, own) if q == 0 else jnp.where(sub3, own, rim)
            load_taps(lhs, taps.at[q], e, tile)
        shift_taps(lhs, shift, taps.at[q], RB + 2)

    def first(d, k, buf):
        sub = lax.broadcasted_iota(jnp.int32, (8, 128), 0)
        base, _, wc = brick_plan(tab, wv, d * BRICKS + k)
        c0 = brick_columns(taps.at[0], base, wc)
        c1 = brick_columns(taps.at[1], base, wc)
        f = tab[3, d * BRICKS + k]
        kw = [kv[f, t] for t in range(4)]
        for i in range(4):
            at = [c0[i]] + [pltpu.roll(jnp.where(sub >= a, c0[i], c1[i]), 8 - a, 0) for a in range(1, 7)]
            near = kw[0] * at[3] + kw[1] * (at[2] + at[4])
            buf[k, i] = near + (kw[2] * (at[1] + at[5]) + kw[3] * (at[0] + at[6]))

    def second(d, k, buf):
        base, wr, wc = brick_plan(tab, wv, d * BRICKS + k)
        c = brick_rows_adjoint(wr, brick_rows(wr, [buf[k, i] for i in range(4)]))
        brick_add(acc, base, wc, c)

    each_peer(first, second, bufs)

    def put(e, block):
        if e == 0:
            lo[...] = block
        elif e == RB + 1:
            hi[...] = block
        else:
            out[:, e - 1] = block

    shift_taps_adjoint(lhs, shift_t, acc, put)


EDGE = jax.ShapeDtypeStruct((PEERS, 8, 128), F32)


def normal(tab, shift, shift_t, x, prv, nxt):
    return pl.pallas_call(
        normal_kernel,
        in_specs=[SMEM, VMEM, VMEM, VMEM, VMEM, VMEM],
        out_specs=[VMEM, VMEM, VMEM],
        out_shape=[turned_shape(), EDGE, EDGE],
        scratch_shapes=[
            pltpu.VMEM((2, 4, PEERS * (RB + 2), 8, 128), F32),
            TAPS,
            WV,
            WV,
            LHS,
            BUF,
            BUF,
        ],
        compiler_params=params(24),
        name="normal",
    )(tab, shift, shift_t, x, prv, nxt)


def depth_matrix(q, transpose):
    n = q // QF
    f = (q % QF).astype(F32) * (1.0 / QF)
    weights = (
        f * (f - 1.0) * (f - 2.0) * (-1.0 / 6.0),
        (f + 1.0) * (f - 1.0) * (f - 2.0) * 0.5,
        (f + 1.0) * f * (f - 2.0) * -0.5,
        (f + 1.0) * f * (f - 1.0) * (1.0 / 6.0),
    )
    i = lax.broadcasted_iota(jnp.int32, (128, 128), 0)
    j = lax.broadcasted_iota(jnp.int32, (128, 128), 1)
    off = (i - j if transpose else j - i) + (257 - n)
    off = jnp.bitwise_and(off, 127)
    w = jnp.zeros((128, 128), F32)
    for m in range(4):
        w = jnp.where(off == m, weights[m], w)
    return w


def depth_product(q, transpose, r, k):
    wh, wl = split(depth_matrix(q, transpose))
    xh, xl = split(jnp.concatenate([r[:, 2 * k + h].reshape(128, 128) for h in range(2)], axis=1))
    y = jnp.dot(
        jnp.concatenate([wh, wl, wh], axis=1), jnp.concatenate([xh, xh, xl], axis=0), preferred_element_type=F32
    )
    return y[:, :128], y[:, 128:]


PACKED = 8 * RB + 6 * RB


def depth_kernel(code, r, a, out):
    sub = lax.broadcasted_iota(jnp.int32, (PEERS, 8, 128), 1)
    for k in range(BRICKS):
        ys = depth_product(code[k], False, r, k)
        for h in range(2):
            rb = 2 * k + h
            tiles = ys[h].reshape(PEERS, 8, 128) + a[:, rb]
            out[:, 8 * rb : 8 * rb + 8] = tiles
            moved = pltpu.roll(tiles, 3, 1)
            before = jnp.concatenate([moved[-1:], moved[:-1]], axis=0)
            after = jnp.concatenate([moved[1:], moved[:1]], axis=0)
            rim = jnp.where(sub < 3, before, after)
            out[:, 8 * RB + 6 * rb : 8 * RB + 6 * rb + 6] = rim[:, :6]


def depth(code, r, a):
    return pl.pallas_call(
        depth_kernel,
        in_specs=[SMEM, VMEM, VMEM],
        out_specs=VMEM,
        out_shape=jax.ShapeDtypeStruct((PEERS, PACKED, 128), F32),
        compiler_params=params(24),
        name="depth",
    )(code, r, a)


def depth_adjoint_kernel(code, r, out):
    for k in range(BRICKS):
        ys = depth_product(code[k], True, r, k)
        for h in range(2):
            out[:, 2 * k + h] = ys[h].reshape(PEERS, 8, 128)


def depth_adjoint(code, r):
    return pl.pallas_call(
        depth_adjoint_kernel,
        in_specs=[SMEM, VMEM],
        out_specs=VMEM,
        out_shape=turned_shape(),
        compiler_params=params(24),
        name="depth_adjoint",
    )(code, r)


def to_next(x, axis, count):
    return lax.ppermute(x, axis, [(i, (i + 1) % count) for i in range(count)])


def to_prev(x, axis, count):
    return lax.ppermute(x, axis, [((i + 1) % count, i) for i in range(count)])


def swap(x):
    return lax.all_to_all(x, "gy", split_axis=0, concat_axis=0, tiled=True)


def brick_table(raw):
    t = raw.astype(jnp.int32)
    slot = t[:, 32:38]
    sends = t[:, :32].reshape(PEERS, PEERS, 2).transpose(1, 0, 2).reshape(PEERS, 1, 32)
    hit = slot[:, :, None] == jnp.arange(32)[None, None, :]
    local = jnp.sum(jnp.where(hit, sends, 0), axis=2)
    rows = [2 * PEERS * local + slot // 2, t[:, 38:44], t[:, 44:50], t[:, 50:56] % QF]
    return jnp.stack(rows).reshape(4, PEERS * BRICKS)


def body(velocity, states, pull_plan, send_plan, codes):
    gx = lax.axis_size("gx")
    gy = lax.axis_size("gy")
    left = to_next(states[:, :, -1], "gy", gy)
    right = to_prev(states[:, :, 0], "gy", gy)
    a0, a1, sides, my_prv, my_nxt = pre(velocity, states)
    shift = jnp.asarray(SHIFT, BF16)
    shift_t = jnp.asarray(SHIFT.T, BF16)
    code = codes[2].reshape(BRICKS)
    mine = [send_plan.reshape(32), pull_plan.reshape(BRICKS), codes.reshape(3 * BRICKS)]
    table = jnp.concatenate([jnp.zeros((32,), jnp.int32)] + mine + [jnp.zeros((40,), jnp.int32)])
    table = table.astype(F32).reshape(1, 128)

    my_prv, my_nxt = rims(my_prv, my_nxt, sides, left, right)
    from_nxt = to_prev(my_prv, "gx", gx)
    from_prv = to_next(my_nxt, "gx", gx)
    a0, a1 = columns(a0, a1, sides, left, right)
    a0, a1 = close(a0, a1, my_prv, my_nxt, from_nxt, from_prv, table)
    a0, code = lax.optimization_barrier((a0, code))
    x = swap(a0)
    tab = brick_table(x[:, RB, 0, 32:88])
    r = swap(pull(tab, shift, x))
    u = swap(depth(code, r, a1))
    low = jnp.concatenate([u[:, 8 * RB - 8 : 8 * RB], u[:, PACKED - 8 :]], axis=1)
    high = jnp.concatenate([u[:, :8], u[:, 8 * RB : 8 * RB + 8]], axis=1)
    y, lo, hi = normal(tab, shift, shift_t, u, to_next(low, "gx", gx), to_prev(high, "gx", gx))
    y = y.at[:, RB - 1].add(to_prev(lo, "gx", gx)).at[:, 0].add(to_next(hi, "gx", gx))
    adj1 = swap(y)
    v = swap(depth_adjoint(code, adj1))
    y, states = push(tab, shift_t, v, states)
    adj0 = swap(y)
    return force(adj1, adj0, states, (from_prv, from_nxt, left, right))


def solution(mesh):
    return jax.shard_map(
        body,
        mesh=mesh,
        in_specs=(
            P(None, "gx", "gy", None),
            P(None, "gx", "gy", None),
            P("gx", "gy"),
            P("gx", "gy", None, None),
            P(None, "gx", "gy"),
        ),
        out_specs=P(None, "gx", "gy", None),
        check_vma=False,
    )
```

```python
import functools

import jax
import jax.numpy as jnp
import numpy as np
from jax import lax
from jax.experimental import pallas as pl
from jax.experimental.pallas import tpu as pltpu
from jax.sharding import PartitionSpec as P

QF = 8
PEERS = 16
RB = 12
BRICKS = 6


def weights_of(f):
    return np.array(
        [
            -f * (f - 1.0) * (f - 2.0) / 6.0,
            (f + 1.0) * (f - 1.0) * (f - 2.0) / 2.0,
            -(f + 1.0) * f * (f - 2.0) / 2.0,
            (f + 1.0) * f * (f - 1.0) / 6.0,
        ]
    )


WEIGHTS = np.stack([weights_of(k / QF) for k in range(QF)])
PAIRS = np.stack([[np.dot(w[: 4 - d], w[d:]) for d in range(4)] for w in WEIGHTS])


def shift_matrix():
    m = np.zeros((2, 8, 16, 3, 8, 16), np.float32)
    for r in range(8):
        for j in range(16):
            for n, d in enumerate((-1, 1, 2)):
                inside = 0 <= j + d < 16
                m[0 if inside else 1, r, (j + d) % 16, n, r, j] = 1.0
    return m.reshape(256, 384)


SHIFT = shift_matrix()
BF16 = jnp.bfloat16

VMEM = pl.BlockSpec(memory_space=pltpu.VMEM)
SMEM = pl.BlockSpec(memory_space=pltpu.SMEM)
F32 = jnp.float32


def params(mib=48):
    return pltpu.CompilerParams(vmem_limit_bytes=mib * 1024 * 1024)


def turned_shape(blocks=RB):
    return jax.ShapeDtypeStruct((PEERS, blocks, 8, 128), F32)


def gradients(st, top, bottom, left, right, rb, k):
    rows = pl.ds(rb * 8, 8)
    x = st[k, rows]
    fixed = isinstance(rb, int)
    before = st[k, max(rb * 8 - 1, 0) if fixed else jnp.maximum(rb * 8 - 1, 0)]
    before = jnp.where(rb == 0, jnp.zeros_like(before) if top is None else top[2 + k], before)
    after = st[k, min(rb * 8 + 8, 95) if fixed else jnp.minimum(rb * 8 + 8, 95)]
    after = jnp.where(rb == RB - 1, jnp.zeros_like(after) if bottom is None else bottom[3 + k], after)
    up = jnp.concatenate([x[1:], after[None]], axis=0)
    down = jnp.concatenate([before[None], x[:-1]], axis=0)
    col = lax.broadcasted_iota(jnp.int32, x.shape, 1)
    lo = 0.0 if left is None else left[k, rows][:, None, :]
    hi = 0.0 if right is None else right[k, rows][:, None, :]
    nxt = jnp.where(col == 15, hi, pltpu.roll(x, 15, 1))
    prv = jnp.where(col == 0, lo, pltpu.roll(x, 1, 1))
    return (
        (up - down) * 0.5,
        (nxt - prv) * 0.5,
        (pltpu.roll(x, 127, 2) - pltpu.roll(x, 1, 2)) * 0.5,
    )


def turn(x):
    return x.reshape(128, 128).T.reshape(PEERS, 8, 128)


def contract(v, g):
    return -0.5 * (v[0] * g[0] + v[1] * g[1] + v[2] * g[2])


CHUNKS = 4


def pre_kernel(v_hbm, st_hbm, out0, out1, sides, to_prv, to_nxt, v, st, sems):
    rows = 96 // CHUNKS
    copies = [pltpu.make_async_copy(st_hbm.at[k], st.at[k], sems.at[k]) for k in range(2)]
    for i in range(CHUNKS):
        part = pl.ds(i * rows, rows)
        copies.append(pltpu.make_async_copy(v_hbm.at[:, part], v.at[:, part], sems.at[2 + i]))
    for c in copies:
        c.start()
    copies[0].wait()
    copies[1].wait()
    for i in range(CHUNKS):
        copies[2 + i].wait()

        for rb in range(i * RB // CHUNKS, (i + 1) * RB // CHUNKS):
            block = pl.ds(rb * 8, 8)
            vb = v[:, block]
            a = contract(vb, gradients(st, None, None, None, None, rb, 0))
            out0[:, rb] = turn(a)
            out1[:, rb] = turn(contract(vb, gradients(st, None, None, None, None, rb, 1)))
            sides[0, block] = 0.25 * vb[1, :, 0]
            sides[1, block] = -0.25 * vb[1, :, 15]

            if rb == 0:
                to_prv[0] = a[0]
                to_prv[2] = a[1]

            if rb == RB - 1:
                to_nxt[0] = a[7]

    to_prv[1] = v[0, 0]
    to_prv[3] = st[0, 0]
    to_prv[4] = st[1, 0]
    to_nxt[1] = v[0, 95]
    to_nxt[2] = st[0, 95]
    to_nxt[3] = st[1, 95]


def in_hbm(x):
    return pltpu.with_memory_space_constraint(x, pltpu.HBM)


def pre(velocity, states):
    hbm = pl.BlockSpec(memory_space=pltpu.HBM)
    return pl.pallas_call(
        pre_kernel,
        in_specs=[hbm, hbm],
        out_specs=[VMEM] * 5,
        out_shape=[
            turned_shape(RB + 1),
            turned_shape(),
            jax.ShapeDtypeStruct((2, 96, 128), F32),
            jax.ShapeDtypeStruct((5, 16, 128), F32),
            jax.ShapeDtypeStruct((4, 16, 128), F32),
        ],
        scratch_shapes=[
            pltpu.VMEM((3, 96, 16, 128), F32),
            pltpu.VMEM((2, 96, 16, 128), F32),
            pltpu.SemaphoreType.DMA((2 + CHUNKS,)),
        ],
        compiler_params=params(24),
        cost_estimate=COST,
        name="pre",
    )(in_hbm(velocity), in_hbm(states))


def rims_kernel(prv, nxt, sides, left, right, to_prv, to_nxt):
    col = lax.broadcasted_iota(jnp.int32, (16, 128), 0)

    def side(row):
        lo = sides[0, row : row + 1] * left[0, row : row + 1]
        hi = sides[1, row : row + 1] * right[0, row : row + 1]
        return jnp.where(col == 0, lo, 0.0) + jnp.where(col == 15, hi, 0.0)

    to_prv[0] = prv[0] + side(0)
    to_prv[1] = prv[1]
    to_prv[2] = prv[2] + side(1)
    to_prv[3] = prv[3]
    to_prv[4] = prv[4]
    to_nxt[0] = nxt[0] + side(95)
    to_nxt[1] = nxt[1]
    to_nxt[2] = nxt[2]
    to_nxt[3] = nxt[3]


def rims(prv, nxt, sides, left, right):
    return pl.pallas_call(
        rims_kernel,
        in_specs=[VMEM] * 5,
        out_specs=[VMEM, VMEM],
        out_shape=[jax.ShapeDtypeStruct((5, 16, 128), F32), jax.ShapeDtypeStruct((4, 16, 128), F32)],
        compiler_params=params(16),
        name="rims",
    )(prv, nxt, sides, left, right)


def columns_kernel(a0, a1, sides, left, right, out0, out1):
    col = lax.broadcasted_iota(jnp.int32, (8, 16, 128), 1)
    for k, (a, out) in enumerate(((a0, out0), (a1, out1))):
        for j in range(3):
            rows = pl.ds(8 * j, 8)
            lo = (sides[0, rows] * left[k, rows])[:, None, :]
            hi = (sides[1, rows] * right[k, rows])[:, None, :]
            out[:, j] = a[:, j] + turn(jnp.where(col == 0, lo, 0.0) + jnp.where(col == 15, hi, 0.0))


def columns(a0, a1, sides, left, right):
    block = pl.BlockSpec((PEERS, 3, 8, 128), lambda i: (0, i, 0, 0))
    side = pl.BlockSpec((2, 24, 128), lambda i: (0, i, 0))
    return pl.pallas_call(
        columns_kernel,
        grid=(RB // 3,),
        in_specs=[block, block, side, side, side],
        out_specs=[block, block],
        out_shape=[turned_shape(RB + 1), turned_shape()],
        input_output_aliases={0: 0, 1: 1},
        compiler_params=params(16),
        cost_estimate=COST,
        name="columns",
    )(a0, a1, sides, left, right)


def whole(shape):
    return pl.BlockSpec(shape, lambda i: (0,) * len(shape))


def natural3(f):
    return pl.BlockSpec((3, 8, 16, 128), lambda i: (0, f(i), 0, 0))


def turned(f):
    return pl.BlockSpec((PEERS, 1, 8, 128), lambda i: (0, f(i), 0, 0))


def same(i):
    return i


COST = pl.CostEstimate(flops=20_000_000, bytes_accessed=6_000_000, transcendentals=0)


def close_kernel(a0, a1, my_prv, my_nxt, from_nxt, from_prv, table, out0, out1):
    i = pl.program_id(0)
    row = lax.broadcasted_iota(jnp.int32, (8, 16, 128), 0)
    zero = jnp.zeros((8, 16, 128), F32)
    lane = lax.broadcasted_iota(jnp.int32, (PEERS, 8, 128), 2)

    @pl.when(i == 0)
    def _():
        for k, (a, out) in enumerate(((a0, out0), (a1, out1))):
            x = 0.25 * my_prv[1] * from_prv[2 + k]
            out[:, 0] = a[:, 0] + turn(jnp.where(row == 0, x[None], zero))

    @pl.when(i == 1)
    def _():
        for k, (a, out) in enumerate(((a0, out0), (a1, out1))):
            x = -0.25 * my_nxt[1] * from_nxt[3 + k]
            out[:, 0] = a[:, 0] + turn(jnp.where(row == 7, x[None], zero))

    @pl.when(i == 2)
    def _():
        before = from_prv[0] - 0.25 * from_prv[1] * my_prv[3]
        after = from_nxt[0] + 0.25 * from_nxt[1] * my_nxt[2]
        x = jnp.where(row == 7, before[None], zero)
        x = jnp.where(row == 0, after[None], x)
        x = jnp.where(row == 1, from_nxt[2][None], x)
        inner = (lane >= 32) & (lane < 112)
        out0[:, 0] = jnp.where(inner, table[...][None], turn(x))


def close(a0, a1, my_prv, my_nxt, from_nxt, from_prv, table):
    def block(i):
        return jnp.minimum(i * (RB - 1), RB)

    def kept(i):
        return jnp.minimum(i * (RB - 1), RB - 1)

    return pl.pallas_call(
        close_kernel,
        grid=(3,),
        in_specs=[
            turned(block),
            turned(kept),
            whole((5, 16, 128)),
            whole((4, 16, 128)),
            whole((5, 16, 128)),
            whole((4, 16, 128)),
            whole((1, 128)),
        ],
        out_specs=[turned(block), turned(kept)],
        out_shape=[turned_shape(RB + 1), turned_shape()],
        input_output_aliases={0: 0, 1: 1},
        compiler_params=params(16),
        name="close",
    )(a0, a1, my_prv, my_nxt, from_nxt, from_prv, table)


def force_block(adj1, adj0, st, edges, rb, out):
    b1 = (adj1.reshape(128, 128).T * -0.5).reshape(8, 16, 128)
    b0 = (adj0.reshape(128, 128).T * -0.5).reshape(8, 16, 128)
    g1 = gradients(st, *edges, rb, 1)
    g0 = gradients(st, *edges, rb, 0)
    for c in range(3):
        out[c] = b1 * g1[c] + b0 * g0[c]


def force_kernel(adj1, adj0, st, top, bottom, left, right, out_hbm, buf, sems):
    copies = []
    for n in range((RB - 2) // 2):
        for rb in (2 * n + 1, 2 * n + 2):
            rows = buf.at[:, pl.ds(8 * rb, 8)]
            force_block(adj1[:, rb], adj0[:, rb], st, (top, bottom, left, right), rb, rows)
        part = pl.ds(16 * n + 8, 16)
        copies.append(pltpu.make_async_copy(buf.at[:, part], out_hbm.at[:, part], sems.at[n]))
        copies[-1].start()
    for c in copies:
        c.wait()


def force_edge_kernel(adj1, adj0, st, top, bottom, left, right, from_nxt, from_prv, prior, out):
    i = pl.program_id(0)
    lane = lax.broadcasted_iota(jnp.int32, (PEERS, 8, 128), 2)
    x = jnp.where((i == 0) & (lane < 32), from_prv[...], 0.0)
    x = x + jnp.where((i == 1) & (lane >= 112), from_nxt[...], 0.0)
    force_block(adj1[:, 0], adj0[:, 0] + x, st, (top, bottom, left, right), i * (RB - 1), out)


def force(adj1, adj0, states, edges):
    fixed = [whole((2, 96, 16, 128)), whole((4, 16, 128)), whole((5, 16, 128)), whole((2, 96, 128)), whole((2, 96, 128))]
    shape = jax.ShapeDtypeStruct((3, 96, 16, 128), F32)
    rim = adj0[:, RB]
    from_nxt = to_prev(rim, "gx", lax.axis_size("gx"))
    from_prv = to_next(rim, "gx", lax.axis_size("gx"))
    args = (adj1, adj0, states, *edges)

    def outer(i):
        return i * (RB - 1)

    main = pl.pallas_call(
        force_kernel,
        in_specs=[VMEM] * 7,
        out_specs=pl.BlockSpec(memory_space=pltpu.HBM),
        out_shape=shape,
        scratch_shapes=[pltpu.VMEM((3, 96, 16, 128), F32), pltpu.SemaphoreType.DMA(((RB - 2) // 2,))],
        compiler_params=params(24),
        cost_estimate=COST,
        name="force",
    )(*args)
    return pl.pallas_call(
        force_edge_kernel,
        grid=(2,),
        in_specs=[turned(outer), turned(outer)]
        + fixed
        + [whole((PEERS, 8, 128)), whole((PEERS, 8, 128)), pl.BlockSpec(memory_space=pl.ANY)],
        out_specs=natural3(outer),
        out_shape=shape,
        input_output_aliases={9: 0},
        compiler_params=params(24),
        name="force_edge",
    )(*args, from_nxt, from_prv, main)


def lanes():
    return lax.broadcasted_iota(jnp.int32, (8, 128), 1)


def split(x):
    hi = x.astype(BF16)
    return hi, (x - hi.astype(F32)).astype(BF16)


def load_taps(lhs, taps, e, x):
    col = lax.broadcasted_iota(jnp.int32, x.shape, 2) % 16
    after = jnp.concatenate([x[1:], x[:1]], axis=0)
    before = jnp.concatenate([x[-1:], x[:-1]], axis=0)
    xh, xl = split(x.reshape(128, 128))
    eh, el = split(jnp.where(col < 2, after, before).reshape(128, 128))
    rows = pl.ds(e * 128, 128)
    lhs[rows, 0:128] = xh
    lhs[rows, 128:256] = eh
    lhs[rows, 256:384] = xl
    lhs[rows, 384:512] = el
    taps[1, pl.ds(e * PEERS, PEERS)] = x


def shift_taps(lhs, shift, taps, blocks):
    m = shift[...]
    y = jnp.dot(lhs[0 : blocks * 128, 0:512], jnp.concatenate([m, m], axis=0), preferred_element_type=F32)
    for n, t in enumerate((0, 2, 3)):
        taps[t, 0 : blocks * PEERS] = y[:, n * 128 : n * 128 + 128].reshape(blocks * PEERS, 8, 128)


def shift_taps_adjoint(lhs, shift_t, acc, put):
    @pl.loop(0, RB + 2)
    def _(e):
        rows = pl.ds(e * 128, 128)
        for n, t in enumerate((0, 2, 3)):
            h, l = split(acc[t, pl.ds(e * PEERS, PEERS)].reshape(128, 128))
            lhs[rows, n * 128 : n * 128 + 128] = h
            lhs[rows, 384 + n * 128 : 512 + n * 128] = l

    m = shift_t[...]
    y = jnp.dot(lhs[...], jnp.concatenate([m, m], axis=0), preferred_element_type=F32)
    col = lax.broadcasted_iota(jnp.int32, (PEERS, 8, 128), 2) % 16
    for e in range(RB + 2):
        own = y[e * 128 : e * 128 + 128, :128].reshape(PEERS, 8, 128)
        rim = y[e * 128 : e * 128 + 128, 128:].reshape(PEERS, 8, 128)
        after = jnp.concatenate([rim[-1:], rim[:-1]], axis=0)
        before = jnp.concatenate([rim[1:], rim[:1]], axis=0)
        put(e, acc[1, e * PEERS : (e + 1) * PEERS] + own + jnp.where(col < 2, after, before))


def fill_weights(wv, values):
    for f in range(QF):
        for t in range(4):
            wv[f, t] = jnp.full((8, 128), float(values[f, t]), F32)


def brick_plan(tab, wv, b):
    base = tab[0, b]
    u = tab[1, b]
    v = tab[2, b]
    return base, [wv[u, t] for t in range(4)], [wv[v, t] for t in range(4)]


def brick_columns(taps, base, wc):
    c = []
    for i in range(4):
        acc = [wc[t] * taps[t, base + i * PEERS] for t in range(4)]
        c.append((acc[0] + acc[1]) + (acc[2] + acc[3]))
    return c


def brick_rows(wr, c):
    lane = lanes()
    outs = []
    for h in range(2):
        prv, cur, nxt = c[h], c[h + 1], c[h + 2]
        outs.append(
            (wr[0] * pltpu.roll(jnp.where(lane >= 112, prv, cur), 16, 1) + wr[1] * cur)
            + (
                wr[2] * pltpu.roll(jnp.where(lane < 16, nxt, cur), 112, 1)
                + wr[3] * pltpu.roll(jnp.where(lane < 32, nxt, cur), 96, 1)
            )
        )
    return outs


def brick_rows_adjoint(wr, v):
    lane = lanes()
    lo, own, hi = [], [], []
    for h in range(2):
        p0 = wr[0] * pltpu.roll(v[h], 112, 1)
        p2 = wr[2] * pltpu.roll(v[h], 16, 1)
        p3 = wr[3] * pltpu.roll(v[h], 32, 1)
        lo.append(jnp.where(lane >= 112, p0, 0.0))
        own.append(
            (wr[1] * v[h] + jnp.where(lane >= 112, 0.0, p0))
            + (jnp.where(lane < 16, 0.0, p2) + jnp.where(lane < 32, 0.0, p3))
        )
        hi.append(jnp.where(lane < 16, p2, 0.0) + jnp.where(lane < 32, p3, 0.0))
    return [lo[0], own[0] + lo[1], own[1] + hi[0], hi[1]]


def brick_add(acc, base, wc, c):
    for i in range(4):
        for t in range(4):
            acc[t, base + i * PEERS] = acc[t, base + i * PEERS] + wc[t] * c[i]


BUF = pltpu.VMEM((BRICKS, 4, 8, 128), F32)


def each_peer(first, second, bufs):
    for k in range(BRICKS):
        first(0, k, bufs[0])

    @pl.loop(0, PEERS // 2)
    def _(i):
        d = 2 * i
        for k in range(BRICKS):
            second(d, k, bufs[0])
            first(d + 1, k, bufs[1])
        for k in range(BRICKS):
            second(d + 1, k, bufs[1])
            first(jnp.minimum(d + 2, PEERS - 1), k, bufs[0])


def pull_kernel(tab, shift, x, out, taps, wv, lhs, *bufs):
    fill_weights(wv, WEIGHTS)
    load_taps(lhs, taps, 0, x[:, RB])

    @pl.loop(0, RB)
    def _(rb):
        load_taps(lhs, taps, rb + 1, x[:, rb])

    shift_taps(lhs, shift, taps, RB + 1)
    for t in range(4):
        taps[t, (RB + 1) * PEERS :] = taps[t, 0:PEERS]

    def first(d, k, buf):
        base, _, wc = brick_plan(tab, wv, d * BRICKS + k)
        c = brick_columns(taps, base, wc)
        for i in range(4):
            buf[k, i] = c[i]

    def second(d, k, buf):
        _, wr, _ = brick_plan(tab, wv, d * BRICKS + k)
        o = brick_rows(wr, [buf[k, i] for i in range(4)])
        for h in range(2):
            out[d, 2 * k + h] = o[h]

    each_peer(first, second, bufs)


TAPS = pltpu.VMEM((4, PEERS * (RB + 2), 8, 128), F32)
WV = pltpu.VMEM((QF, 4, 8, 128), F32)


LHS = pltpu.VMEM(((RB + 2) * 128, 768), BF16)


def pull(tab, shift, x):
    return pl.pallas_call(
        pull_kernel,
        in_specs=[SMEM, VMEM, VMEM],
        out_specs=VMEM,
        out_shape=turned_shape(),
        scratch_shapes=[TAPS, WV, LHS, BUF, BUF],
        compiler_params=params(24),
        name="pull",
    )(tab, shift, x)


def clear(acc):
    @pl.loop(0, RB + 2)
    def _(e):
        acc[:, pl.ds(e * PEERS, PEERS)] = jnp.zeros((4, PEERS, 8, 128), F32)


def push_kernel(tab, shift_t, v, st_hbm, out, st, acc, wv, lhs, buf_a, buf_b, sem):
    copy = pltpu.make_async_copy(st_hbm, st, sem)
    copy.start()
    fill_weights(wv, WEIGHTS)
    clear(acc)

    def first(d, k, buf):
        _, wr, _ = brick_plan(tab, wv, d * BRICKS + k)
        c = brick_rows_adjoint(wr, [v[d, 2 * k], v[d, 2 * k + 1]])
        for i in range(4):
            buf[k, i] = c[i]

    def second(d, k, buf):
        base, _, wc = brick_plan(tab, wv, d * BRICKS + k)
        brick_add(acc, base, wc, [buf[k, i] for i in range(4)])

    each_peer(first, second, (buf_a, buf_b))

    def put(e, block):
        if e == 0:
            out[:, RB] = block
        elif e == RB + 1:
            out[:, RB] = out[:, RB] + block
        else:
            out[:, e - 1] = block

    shift_taps_adjoint(lhs, shift_t, acc, put)
    copy.wait()


def push(tab, shift_t, v, states):
    return pl.pallas_call(
        push_kernel,
        in_specs=[SMEM, VMEM, VMEM, pl.BlockSpec(memory_space=pltpu.HBM)],
        out_specs=[VMEM, VMEM],
        out_shape=[turned_shape(RB + 1), jax.ShapeDtypeStruct(states.shape, F32)],
        scratch_shapes=[TAPS, WV, LHS, BUF, BUF, pltpu.SemaphoreType.DMA],
        compiler_params=params(24),
        name="push",
    )(tab, shift_t, v, in_hbm(states))


def normal_kernel(tab, shift, shift_t, x, prv, nxt, out, lo, hi, taps, acc, wv, kv, lhs, *bufs):
    fill_weights(wv, WEIGHTS)
    fill_weights(kv, PAIRS)
    clear(acc)
    sub3 = lax.broadcasted_iota(jnp.int32, (PEERS, 8, 128), 1) < 3
    last = 8 * RB + 6 * (RB - 1) - 2

    def block(e):
        if e == 0:
            return prv[:, 0:8], pltpu.roll(prv[:, 8:16], 6, 1)
        if e == RB + 1:
            return nxt[:, 0:8], nxt[:, 8:16]
        if e == RB:
            return x[:, 8 * RB - 8 : 8 * RB], pltpu.roll(x[:, last : last + 8], 6, 1)
        return x[:, 8 * e - 8 : 8 * e], x[:, 8 * RB + 6 * (e - 1) : 8 * RB + 6 * (e - 1) + 8]

    for q in range(2):
        for e in range(RB + 2):
            own, rim = block(e)
            own = pltpu.roll(own, 3, 1)
            tile = jnp.where(sub3, rim, own) if q == 0 else jnp.where(sub3, own, rim)
            load_taps(lhs, taps.at[q], e, tile)
        shift_taps(lhs, shift, taps.at[q], RB + 2)

    def first(d, k, buf):
        sub = lax.broadcasted_iota(jnp.int32, (8, 128), 0)
        base, _, wc = brick_plan(tab, wv, d * BRICKS + k)
        c0 = brick_columns(taps.at[0], base, wc)
        c1 = brick_columns(taps.at[1], base, wc)
        f = tab[3, d * BRICKS + k]
        kw = [kv[f, t] for t in range(4)]
        for i in range(4):
            at = [c0[i]] + [pltpu.roll(jnp.where(sub >= a, c0[i], c1[i]), 8 - a, 0) for a in range(1, 7)]
            near = kw[0] * at[3] + kw[1] * (at[2] + at[4])
            buf[k, i] = near + (kw[2] * (at[1] + at[5]) + kw[3] * (at[0] + at[6]))

    def second(d, k, buf):
        base, wr, wc = brick_plan(tab, wv, d * BRICKS + k)
        c = brick_rows_adjoint(wr, brick_rows(wr, [buf[k, i] for i in range(4)]))
        brick_add(acc, base, wc, c)

    each_peer(first, second, bufs)

    def put(e, block):
        if e == 0:
            lo[...] = block
        elif e == RB + 1:
            hi[...] = block
        else:
            out[:, e - 1] = block

    shift_taps_adjoint(lhs, shift_t, acc, put)


EDGE = jax.ShapeDtypeStruct((PEERS, 8, 128), F32)


def normal(tab, shift, shift_t, x, prv, nxt):
    return pl.pallas_call(
        normal_kernel,
        in_specs=[SMEM, VMEM, VMEM, VMEM, VMEM, VMEM],
        out_specs=[VMEM, VMEM, VMEM],
        out_shape=[turned_shape(), EDGE, EDGE],
        scratch_shapes=[
            pltpu.VMEM((2, 4, PEERS * (RB + 2), 8, 128), F32),
            TAPS,
            WV,
            WV,
            LHS,
            BUF,
            BUF,
        ],
        compiler_params=params(24),
        name="normal",
    )(tab, shift, shift_t, x, prv, nxt)


def depth_matrix(q, transpose):
    n = q // QF
    f = (q % QF).astype(F32) * (1.0 / QF)
    weights = (
        f * (f - 1.0) * (f - 2.0) * (-1.0 / 6.0),
        (f + 1.0) * (f - 1.0) * (f - 2.0) * 0.5,
        (f + 1.0) * f * (f - 2.0) * -0.5,
        (f + 1.0) * f * (f - 1.0) * (1.0 / 6.0),
    )
    i = lax.broadcasted_iota(jnp.int32, (128, 128), 0)
    j = lax.broadcasted_iota(jnp.int32, (128, 128), 1)
    off = (i - j if transpose else j - i) + (257 - n)
    off = jnp.bitwise_and(off, 127)
    w = jnp.zeros((128, 128), F32)
    for m in range(4):
        w = jnp.where(off == m, weights[m], w)
    return w


def depth_product(q, transpose, r, k):
    wh, wl = split(depth_matrix(q, transpose))
    xh, xl = split(jnp.concatenate([r[:, 2 * k + h].reshape(128, 128) for h in range(2)], axis=1))
    y = jnp.dot(
        jnp.concatenate([wh, wl, wh], axis=1), jnp.concatenate([xh, xh, xl], axis=0), preferred_element_type=F32
    )
    return y[:, :128], y[:, 128:]


PACKED = 8 * RB + 6 * RB


def depth_kernel(code, r, a, out):
    sub = lax.broadcasted_iota(jnp.int32, (PEERS, 8, 128), 1)
    for k in range(BRICKS):
        ys = depth_product(code[k], False, r, k)
        for h in range(2):
            rb = 2 * k + h
            tiles = ys[h].reshape(PEERS, 8, 128) + a[:, rb]
            out[:, 8 * rb : 8 * rb + 8] = tiles
            moved = pltpu.roll(tiles, 3, 1)
            before = jnp.concatenate([moved[-1:], moved[:-1]], axis=0)
            after = jnp.concatenate([moved[1:], moved[:1]], axis=0)
            rim = jnp.where(sub < 3, before, after)
            out[:, 8 * RB + 6 * rb : 8 * RB + 6 * rb + 6] = rim[:, :6]


def depth(code, r, a):
    return pl.pallas_call(
        depth_kernel,
        in_specs=[SMEM, VMEM, VMEM],
        out_specs=VMEM,
        out_shape=jax.ShapeDtypeStruct((PEERS, PACKED, 128), F32),
        compiler_params=params(24),
        name="depth",
    )(code, r, a)


def depth_adjoint_kernel(code, r, out):
    for k in range(BRICKS):
        ys = depth_product(code[k], True, r, k)
        for h in range(2):
            out[:, 2 * k + h] = ys[h].reshape(PEERS, 8, 128)


def depth_adjoint(code, r):
    return pl.pallas_call(
        depth_adjoint_kernel,
        in_specs=[SMEM, VMEM],
        out_specs=VMEM,
        out_shape=turned_shape(),
        compiler_params=params(24),
        name="depth_adjoint",
    )(code, r)


def to_next(x, axis, count):
    return lax.ppermute(x, axis, [(i, (i + 1) % count) for i in range(count)])


def to_prev(x, axis, count):
    return lax.ppermute(x, axis, [((i + 1) % count, i) for i in range(count)])


def swap(x):
    return lax.all_to_all(x, "gy", split_axis=0, concat_axis=0, tiled=True)


def brick_table(raw):
    t = raw.astype(jnp.int32)
    slot = t[:, 32:38]
    sends = t[:, :32].reshape(PEERS, PEERS, 2).transpose(1, 0, 2).reshape(PEERS, 1, 32)
    hit = slot[:, :, None] == jnp.arange(32)[None, None, :]
    local = jnp.sum(jnp.where(hit, sends, 0), axis=2)
    rows = [2 * PEERS * local + slot // 2, t[:, 38:44], t[:, 44:50], t[:, 50:56] % QF]
    return jnp.stack(rows).reshape(4, PEERS * BRICKS)


def body(velocity, states, pull_plan, send_plan, codes):
    gx = lax.axis_size("gx")
    gy = lax.axis_size("gy")
    left = to_next(states[:, :, -1], "gy", gy)
    right = to_prev(states[:, :, 0], "gy", gy)
    a0, a1, sides, my_prv, my_nxt = pre(velocity, states)
    shift = jnp.asarray(SHIFT, BF16)
    shift_t = jnp.asarray(SHIFT.T, BF16)
    code = codes[2].reshape(BRICKS)
    mine = [send_plan.reshape(32), pull_plan.reshape(BRICKS), codes.reshape(3 * BRICKS)]
    table = jnp.concatenate([jnp.zeros((32,), jnp.int32)] + mine + [jnp.zeros((40,), jnp.int32)])
    table = table.astype(F32).reshape(1, 128)

    my_prv, my_nxt = rims(my_prv, my_nxt, sides, left, right)
    from_nxt = to_prev(my_prv, "gx", gx)
    from_prv = to_next(my_nxt, "gx", gx)
    a0, a1 = columns(a0, a1, sides, left, right)
    a0, a1 = close(a0, a1, my_prv, my_nxt, from_nxt, from_prv, table)
    a0, code = lax.optimization_barrier((a0, code))
    x = swap(a0)
    tab = brick_table(x[:, RB, 0, 32:88])
    r = swap(pull(tab, shift, x))
    u = swap(depth(code, r, a1))
    low = jnp.concatenate([u[:, 8 * RB - 8 : 8 * RB], u[:, PACKED - 8 :]], axis=1)
    high = jnp.concatenate([u[:, :8], u[:, 8 * RB : 8 * RB + 8]], axis=1)
    y, lo, hi = normal(tab, shift, shift_t, u, to_next(low, "gx", gx), to_prev(high, "gx", gx))
    y = y.at[:, RB - 1].add(to_prev(lo, "gx", gx)).at[:, 0].add(to_next(hi, "gx", gx))
    adj1 = swap(y)
    v = swap(depth_adjoint(code, adj1))
    y, states = push(tab, shift_t, v, states)
    adj0 = swap(y)
    return force(adj1, adj0, states, (from_prv, from_nxt, left, right))


def solution(mesh):
    return jax.shard_map(
        body,
        mesh=mesh,
        in_specs=(
            P(None, "gx", "gy", None),
            P(None, "gx", "gy", None),
            P("gx", "gy"),
            P("gx", "gy", None, None),
            P(None, "gx", "gy"),
        ),
        out_specs=P(None, "gx", "gy", None),
        check_vma=False,
    )
```
